32 devices in a mesh: visit: 4 (over z), patch: 8 (over y, x, core).
Axes of the slice: x: 2, y: 2, z: 4, core: 2. Of those that a mesh axis runs over, the one named last changes fastest.
Arguments:
- warped_tiles: bfloat16 [1024, 256, 256], P(('visit', 'patch')), may hold values from -6 to 6
- tile_weights: bfloat16 [1024], P(('visit', 'patch')), may hold values from 1 to 9984
- kernel_taps: bfloat16 [1024, 2, 15], P(('visit', 'patch')), may hold values from -3 to 3
- patch_routes: int32 [1024, 1], P(('visit', 'patch')), may hold values from 0 to 7; in each aligned block of 32 rows (0 to 31, 32 to 63, ...) at most 8 rows name the same one
Outputs:
- difference: bfloat16 [1024, 256, 256], P(('visit', 'patch'))
- coadd_image: bfloat16 [8, 256, 256], P('patch')
The draws below stay inside these ranges and needn't reach their ends.
Inputs may be any that keep to these rules, and one draw needn't show every extreme that they name: `patch_routes`: among the 32 rows of one device no patch is named more than 8 times, a bound that some block reaches; every patch is named by some row.
All inputs are finite; a program needn't handle non-finite values.
Results may differ from the reference program's by a relative error of at most 0.0046.
Values may be sent and summed in bfloat16 or wider, within the bound.
A program may use at most 128 MiB of HBM per device.

```python
import math
import jax
import jax.numpy as jnp
import numpy as np
from jax import lax

TILE = 256
KERNEL = 15
TILE_DEV = 32
SLOT_CAP = 8
PATCHES = 8
TILES = 1024


def level_of(rng, dims, split, low, largest):
    level, own = 1.0, jax.random.fold_in(rng, 6)
    for position, parts in split:
        draws = jnp.exp(jax.random.uniform(jax.random.fold_in(own, position), (parts,), jnp.float32, low / len(split), largest / len(split)))
        level = level * jnp.repeat(draws, dims[position] // parts).reshape([-1 if axis == position else 1 for axis in range(len(dims))])
    return level


def routed_block(rng, own, number, rows, amount, top, most, lean):
    order = jax.random.permutation(rng, amount)
    heavy_load, usual = portions_of(amount, rows * top, most, lean, True), portions_of(amount, rows * top, most, lean, False)
    places = jnp.arange(amount)

    def named(sizes, rotation):
        used = int((sizes > 0).sum())
        fixed = max(1, used // 4)
        passed = fixed + (places - fixed + rotation * (used - fixed)) % max(1, amount - fixed)
        return jnp.zeros((amount,), jnp.int32).at[order[jnp.where(places < fixed, places, passed)]].set(jnp.asarray(sizes, jnp.int32))

    sizes = jnp.where(number % 4 == 0, named(heavy_load, number // 4), named(usual, number - number // 4 - 1))
    mixed = jax.random.permutation(jax.random.fold_in(own, 3), amount)
    source_of, taker = mixed[0:amount // 2 * 2:2], mixed[1:amount // 2 * 2:2]
    margin = jnp.minimum(sizes[source_of] - 1, most - sizes[taker]) // 2
    margin = jnp.where((source_of == order[0]) | (taker == order[0]) | (sizes[taker] == 0), 0, jnp.maximum(margin, 0))
    passed = jax.random.randint(jax.random.fold_in(own, 4), (amount // 2,), 0, 1 << 20) % (margin + 1)
    sizes = sizes.at[source_of].add(-passed).at[taker].add(passed)
    members = jnp.searchsorted(jnp.cumsum(sizes), jnp.arange(rows * top), side="right").astype(jnp.int32)
    grid = members.reshape(top, rows).T
    grid = grid[jax.random.permutation(jax.random.fold_in(own, 1), rows)]
    rotation = jax.random.randint(jax.random.fold_in(own, 2), (rows, 1), 0, top)
    return jnp.take_along_axis(grid, (jnp.arange(top)[None, :] + rotation) % top, axis=1)


def portions_of(amount, total, bound, lean, full):
    portions = [(1 << 20) // math.isqrt(grade ** lean) + 1 for grade in range(1, amount + 1)]
    largest = bound if full else min(bound, max(-(-total // amount), total * portions[0] // sum(portions)))
    least = 1 if total - largest >= amount - 1 else 0
    holding, rest = [largest] + [least] * (amount - 1), total - largest - least * (amount - 1)
    while rest > 0:
        movable = [i for i in range(1, amount) if holding[i] < largest] or [i for i in range(1, amount) if holding[i] < bound]
        pool, remaining = sum([portions[i] for i in movable]), rest
        for i in movable:
            extra = min(bound - holding[i], max(1, remaining * portions[i] // pool), rest)
            holding[i] = holding[i] + extra
            rest = rest - extra
    return np.array(holding)


def centred(key, shape, width, limit, split=(), kind=jnp.bfloat16):
    drawn = jax.random.normal(key, shape, jnp.float32) * width
    if len(split) > 0:
        drawn = level_of(key, shape, split, -0.22, 0.18) * drawn
    return jnp.clip(drawn, min=-limit, max=limit).astype(kind)


def setup_inputs(seed: int = 0) -> dict:
    key_of = jax.random.split(jax.random.key(seed), 5)
    warped_tiles = centred(key_of[0], (TILES, TILE, TILE), 1.0, 6.0, ((0, 32),))
    tile_weights = jnp.clip(jnp.exp(math.log(9984.0) - 9.208739 * jax.random.uniform(key_of[1], (TILES,), jnp.float32) ** level_of(key_of[1], (TILES,), ((0, 32),), -0.2, 0.2)), 1.0, 9984.0).astype(jnp.bfloat16)
    kernel_taps = centred(key_of[2], (TILES, 2, KERNEL), 0.4, 3.0, ((0, 32),))
    patch_routes_keys = jax.random.split(jax.random.fold_in(key_of[3], 1), TILES // TILE_DEV)
    patch_routes_turns = jax.random.permutation(jax.random.fold_in(key_of[3], 3), TILES // TILE_DEV)
    patch_routes = jax.vmap(lambda own, number: routed_block(jax.random.fold_in(key_of[3], 2), own, number, TILE_DEV, PATCHES, 1, SLOT_CAP, 2))(patch_routes_keys, patch_routes_turns).reshape((TILES, 1))
    return dict(warped_tiles=warped_tiles, tile_weights=tile_weights, kernel_taps=kernel_taps, patch_routes=patch_routes)


def shift_table(tile_side, kernel):
    rows = jnp.arange(tile_side, dtype=jnp.int32)
    offsets = (rows[None, :] - rows[:, None] + kernel // 2).reshape(-1)
    return (offsets[None, :] == jnp.arange(kernel, dtype=jnp.int32)[:, None]).astype(jnp.bfloat16)


def banded(taps_rows, table, tile_side):
    flat = jnp.dot(taps_rows, table, preferred_element_type=jnp.float32).astype(jnp.bfloat16)
    return flat.reshape(taps_rows.shape[0], tile_side, tile_side)


def match_psf(taps_block, coadd_block, table, tile_side):
    row_bands = banded(taps_block[:, 0, :], table, tile_side)
    col_bands = banded(taps_block[:, 1, :], table, tile_side)
    row_pass = jnp.einsum("nij,njk->nik", row_bands.astype(jnp.float32), coadd_block.astype(jnp.float32)).astype(jnp.bfloat16)
    return jnp.einsum("nik,nlk->nil", row_pass.astype(jnp.float32), col_bands.astype(jnp.float32)).astype(jnp.bfloat16)


def reference(warped_tiles, tile_weights, kernel_taps, patch_routes):
    target = patch_routes[:, 0]
    route_hot = jnp.arange(PATCHES, dtype=jnp.int32)[:, None] == target[None, :]
    weighted_hot = jnp.where(route_hot, tile_weights[None, :], jnp.zeros((), jnp.bfloat16))
    coadd_sum = jnp.dot(weighted_hot, warped_tiles.reshape(TILES, TILE * TILE), preferred_element_type=jnp.float32)
    weight_total = jnp.sum(jnp.where(route_hot, tile_weights[None, :].astype(jnp.float32), jnp.float32(0.0)), axis=1)
    coadd_image = (coadd_sum / weight_total[:, None]).astype(jnp.bfloat16).reshape(PATCHES, TILE, TILE)
    table = shift_table(TILE, KERNEL)
    blocks = TILES // TILE_DEV

    def one_block(packed):
        tile_block, taps_block, target_block = packed
        chosen = coadd_image[target_block]
        template = match_psf(taps_block, chosen, table, TILE)
        return (tile_block.astype(jnp.float32) - template.astype(jnp.float32)).astype(jnp.bfloat16)

    difference = lax.map(one_block, (warped_tiles.reshape(blocks, TILE_DEV, TILE, TILE), kernel_taps.reshape(blocks, TILE_DEV, 2, KERNEL), target.reshape(blocks, TILE_DEV)))
    return difference.reshape(TILES, TILE, TILE), coadd_image
```

```python
import functools
import jax
import jax.numpy as jnp
from jax import lax
from jax.experimental import pallas as pl
from jax.experimental.pallas import tpu as pltpu
from jax.sharding import PartitionSpec as P


def sum_kernel(routes, weights, tiles, part, totals, acc):
    acc[...] = jnp.zeros_like(acc)
    scales = weights[...].astype(jnp.float32)
    for t in range(tiles.shape[0]):
        acc[routes[t]] += tiles[t].astype(jnp.float32) * scales[0:1, t : t + 1]
    part[...] = acc[...].astype(part.dtype)

    @pl.when(pl.program_id(0) == 0)
    def _():
        totals[...] = jnp.zeros_like(totals)
        for t in range(tiles.shape[0]):
            totals[routes[t]] += jnp.broadcast_to(scales[0:1, t : t + 1], totals.shape[1:])


def local_sums(tiles, weights, routes, patches, chunk, dtype):
    count, side, _ = tiles.shape
    return pl.pallas_call(
        sum_kernel,
        grid_spec=pltpu.PrefetchScalarGridSpec(
            num_scalar_prefetch=1,
            grid=(side // chunk,),
            in_specs=[
                pl.BlockSpec(weights.shape, lambda i, *_: (0, 0)),
                pl.BlockSpec((count, chunk, side), lambda i, *_: (0, i, 0)),
            ],
            out_specs=[
                pl.BlockSpec((patches, chunk, side), lambda i, *_: (0, i, 0)),
                pl.BlockSpec((patches, 8, 128), lambda i, *_: (0, 0, 0)),
            ],
            scratch_shapes=[pltpu.VMEM((patches, chunk, side), jnp.float32)],
        ),
        out_shape=[
            jax.ShapeDtypeStruct((patches, side, side), dtype),
            jax.ShapeDtypeStruct((patches, 8, 128), jnp.float32),
        ],
        name="local_sums",
    )(routes, weights, tiles)


def band(row):
    half = 128
    ring = pltpu.roll(jnp.broadcast_to(row, (half, half)), 0, 1, stride=1, stride_axis=0)
    gap = lax.broadcasted_iota(jnp.int32, (half, half), 1) - lax.broadcasted_iota(jnp.int32, (half, half), 0)
    zero = jnp.zeros_like(ring)
    near = jnp.where((gap < 64) & (gap > -64), ring, zero).astype(jnp.bfloat16)
    upper = jnp.where(gap <= -64, ring, zero).astype(jnp.bfloat16)
    lower = jnp.where(gap >= 64, ring, zero).astype(jnp.bfloat16)
    return jnp.concatenate(
        [jnp.concatenate([near, upper], axis=1), jnp.concatenate([lower, near], axis=1)], axis=0
    )


def match_kernel(kernel, routes, taps, tiles, coadd, out, own, rings):
    step = pl.program_id(0)
    group = tiles.shape[0]

    @pl.when(step == 0)
    def _():
        tap = lax.broadcasted_iota(jnp.int32, (kernel, 128), 0)
        lane = lax.broadcasted_iota(jnp.int32, (kernel, 128), 1)
        reach = kernel // 2
        gap = jnp.where(lane >= 64, lane - 128, lane)
        for side, hot in enumerate((tap == reach + gap, tap == reach - gap)):
            rings[side] = lax.dot_general(
                taps[:, side, :], hot.astype(jnp.float32).astype(jnp.bfloat16), (((0,), (0,)), ((), ())),
                preferred_element_type=jnp.float32)
        own[0] = coadd[lax.axis_index("patch")]

    places = [step * group + g for g in range(group)]
    row_passes = [
        jnp.dot(
            band(rings[0, pl.ds(place, 1), :]), coadd[routes[place]], preferred_element_type=jnp.float32
        ).astype(jnp.bfloat16)
        for place in places
    ]
    for g, place in enumerate(places):
        template = jnp.dot(
            row_passes[g], band(rings[1, pl.ds(place, 1), :]), preferred_element_type=jnp.float32
        ).astype(jnp.bfloat16)
        out[g] = (tiles[g].astype(jnp.float32) - template.astype(jnp.float32)).astype(out.dtype)


def subtract(tiles, taps, routes, coadd, group):
    count, side, _ = tiles.shape
    kernel = taps.shape[2]
    flat = taps.transpose(2, 1, 0)
    return pl.pallas_call(
        functools.partial(match_kernel, kernel),
        grid_spec=pltpu.PrefetchScalarGridSpec(
            num_scalar_prefetch=1,
            grid=(count // group,),
            in_specs=[
                pl.BlockSpec(flat.shape, lambda i, *_: (0, 0, 0)),
                pl.BlockSpec((group, side, side), lambda i, *_: (i, 0, 0)),
                pl.BlockSpec(coadd.shape, lambda i, *_: (0, 0, 0)),
            ],
            out_specs=[
                pl.BlockSpec((group, side, side), lambda i, *_: (i, 0, 0)),
                pl.BlockSpec((1, side, side), lambda i, *_: (0, 0, 0)),
            ],
            scratch_shapes=[pltpu.VMEM((2, count, 128), jnp.float32)],
        ),
        out_shape=[
            jax.ShapeDtypeStruct(tiles.shape, jnp.bfloat16),
            jax.ShapeDtypeStruct((1, side, side), jnp.bfloat16),
        ],
        compiler_params=pltpu.CompilerParams(vmem_limit_bytes=24 << 20),
        name="subtract",
    )(routes, flat, tiles, coadd)


def merge_kernel(chips, visits, part, totals, coadd, half, chip_sum, inbox, lane_sum, lane_in, mine,
                 tot_in, tot_mid, tot_z, core_s, core_r, chip_s, chip_r, lane_s, lane_r,
                 back_s, back_r, fan_s, fan_r, pair_s, pair_r, tot_s, tot_r, totz_s, totz_r):
    v = lax.axis_index("visit")
    p = lax.axis_index("patch")
    k, c = p // 2, p % 2
    patches = 2 * chips
    side = part.shape[2]
    rows = side // visits
    sibling = 2 * k + 1 - c

    def span(r):
        return pl.ds(pl.multiple_of(r * rows, rows), rows)

    def remote(src, dst, send, recv, visit, patch):
        return pltpu.make_async_remote_copy(
            src_ref=src, dst_ref=dst, send_sem=send, recv_sem=recv,
            device_id=(visit, patch), device_id_type=pl.DeviceIdType.MESH)

    def chip_at(o):
        return lax.rem(k + o, chips)

    def visit_at(o):
        return lax.rem(v + o, visits)

    def loop(low, high, body):
        if (high - low) <= 4:
            for i in range(low, high):
                body(i)
        else:
            lax.fori_loop(low, high, lambda i, _: (body(i), 0)[1], 0)

    def core_copy(j, r):
        return remote(part.at[j, 1 - c, span(r)], half.at[j, span(r)], core_s.at[j, r], core_r.at[j, r], v, sibling)

    def chip_copy(j, slot, r):
        return remote(chip_sum.at[j, span(r)], inbox.at[slot, span(r)], chip_s.at[j, r], chip_r.at[slot, r], v, 2 * j + c)

    def lane_copy(u, slot):
        return remote(lane_sum.at[u], lane_in.at[slot], lane_s.at[u], lane_r.at[slot], u, p)

    def tot_copy(q, slot):
        return remote(totals.at[q], tot_in.at[slot], tot_s.at[q], tot_r.at[slot], v, q)

    def totz_copy(u, slot):
        return remote(tot_mid, tot_z.at[slot], totz_s.at[u], totz_r.at[slot], u, p)

    def back_copy(u, r):
        piece = coadd.at[p, span(r)]
        return remote(piece, piece, back_s.at[u], back_r.at[r], u, p)

    def fan_copy(j, slot, r):
        piece = coadd.at[2 * slot + c, span(r)]
        return remote(piece, piece, fan_s.at[j, r], fan_r.at[slot, r], v, 2 * j + c)

    def pair_copy(j, core, r):
        piece = coadd.at[2 * j + core, span(r)]
        return remote(piece, piece, pair_s.at[j, r], pair_r.at[j, r], v, sibling)

    barrier = pltpu.get_barrier_semaphore()

    def greet_patch(o):
        pl.semaphore_signal(barrier, inc=1, device_id=(v, lax.rem(p + o, patches)), device_id_type=pl.DeviceIdType.MESH)

    def greet_visit(o):
        pl.semaphore_signal(barrier, inc=1, device_id=(visit_at(o), p), device_id_type=pl.DeviceIdType.MESH)

    loop(1, patches, greet_patch)
    loop(1, visits, greet_visit)
    pl.semaphore_wait(barrier, patches - 1 + visits - 1)

    def start_core(i):
        r = visit_at(i + 1)
        loop(1, chips + 1, lambda o: core_copy(chip_at(o), r).start())

    loop(0, visits, start_core)

    def start_tot(o):
        tot_copy(lax.rem(p + o, patches), p).start()

    loop(1, patches, start_tot)

    def send_chips(i):
        r = visit_at(i + 1)

        def one(o):
            j = chip_at(o)
            core_copy(j, r).wait_recv()
            chip_sum[j, span(r)] = (
                part[j, c, span(r)].astype(jnp.float32) + half[j, span(r)].astype(jnp.float32)
            ).astype(jnp.bfloat16)
            chip_copy(j, k, r).start()

        loop(1, chips, one)

    loop(0, visits, send_chips)

    tot_mid[...] = totals[p]

    def add_tot(o):
        q = lax.rem(p + o, patches)
        tot_copy(q, q).wait_recv()
        tot_mid[...] += tot_in[q]

    loop(1, patches, add_tot)
    loop(1, visits, lambda o: totz_copy(visit_at(o), v).start())

    def gather(r):
        core_copy(k, r).wait_recv()
        mine[...] = part[k, c, span(r)].astype(jnp.float32) + half[k, span(r)].astype(jnp.float32)

        def one(o):
            j = chip_at(o)
            chip_copy(j, j, r).wait_recv()
            mine[...] += inbox[j, span(r)].astype(jnp.float32)

        loop(1, chips, one)

    def send_lane(i):
        r = visit_at(i)
        gather(r)
        lane_sum[r] = mine[...].astype(jnp.bfloat16)
        lane_copy(r, v).start()

    loop(1, visits, send_lane)
    gather(v)
    tot_z[v] = tot_mid[...]

    def add_lane(o):
        u = visit_at(o)
        lane_copy(u, u).wait_recv()
        mine[...] += lane_in[u].astype(jnp.float32)
        totz_copy(u, u).wait_recv()
        tot_z[v] += tot_z[u]

    loop(1, visits, add_lane)
    coadd[p, span(v)] = (mine[...] / tot_z[v][0:1, 0:1]).astype(jnp.bfloat16)

    loop(1, visits, lambda o: back_copy(visit_at(o), v).start())

    def fan_out(r):
        loop(1, chips, lambda o: fan_copy(chip_at(o), k, r).start())
        pair_copy(k, c, r).start()

    def forward(r):
        def one(o):
            j = chip_at(o)
            fan_copy(j, j, r).wait_recv()
            pair_copy(j, c, r).start()

        loop(1, chips, one)

    fan_out(v)

    def relay(i):
        r = visit_at(i)
        back_copy(r, r).wait_recv()
        fan_out(r)
        forward(visit_at(i - 1))

    loop(1, visits, relay)
    forward(visit_at(visits - 1))

    def finish(i):
        def one(o):
            j = chip_at(o)
            pair_copy(j, 1 - c, i).wait_recv()
            pair_copy(j, c, i).wait_send()
            core_copy(j, i).wait_send()

        def peer(o):
            j = chip_at(o)
            chip_copy(j, k, i).wait_send()
            fan_copy(j, k, i).wait_send()

        loop(0, chips, one)
        loop(1, chips, peer)

    loop(0, visits, finish)

    def finish_visit(o):
        u = visit_at(o)
        lane_copy(u, v).wait_send()
        totz_copy(u, v).wait_send()
        back_copy(u, v).wait_send()

    loop(1, visits, finish_visit)
    loop(1, patches, lambda o: tot_copy(lax.rem(p + o, patches), p).wait_send())


def merge(part, totals, patches, visits):
    side = part.shape[1]
    chips = patches // 2
    rows = side // visits
    dma = pltpu.SemaphoreType.DMA
    block = pl.BlockSpec(memory_space=pltpu.VMEM)
    pairs = [dma((chips, visits))] * 2
    return pl.pallas_call(
        functools.partial(merge_kernel, chips, visits),
        in_specs=[block, block],
        out_specs=block,
        out_shape=jax.ShapeDtypeStruct((patches, side, side), jnp.bfloat16),
        scratch_shapes=[
            pltpu.VMEM((chips, side, side), jnp.bfloat16),
            pltpu.VMEM((chips, side, side), jnp.bfloat16),
            pltpu.VMEM((chips, side, side), jnp.bfloat16),
            pltpu.VMEM((visits, rows, side), jnp.bfloat16),
            pltpu.VMEM((visits, rows, side), jnp.bfloat16),
            pltpu.VMEM((rows, side), jnp.float32),
            pltpu.VMEM((patches, 8, 128), jnp.float32),
            pltpu.VMEM((8, 128), jnp.float32),
            pltpu.VMEM((visits, 8, 128), jnp.float32),
        ] + pairs + pairs + [dma((visits,))] * 4 + pairs + pairs + [dma((patches,))] * 2 + [dma((visits,))] * 2,
        compiler_params=pltpu.CompilerParams(collective_id=0, has_side_effects=True),
        name="merge",
    )(part.reshape(chips, 2, side, side), totals)


def local(warped_tiles, tile_weights, kernel_taps, patch_routes):
    patches = lax.axis_size("patch")
    side = warped_tiles.shape[1]
    routes = patch_routes[:, 0]
    part, totals = local_sums(warped_tiles, tile_weights[None, :], routes, patches, 64, jnp.bfloat16)
    coadd = merge(part, totals, patches, lax.axis_size("visit"))
    return tuple(subtract(warped_tiles, kernel_taps, routes, coadd, 16))


def solution(mesh):
    in_specs = (
        P(("visit", "patch"), None, None),
        P(("visit", "patch")),
        P(("visit", "patch"), None, None),
        P(("visit", "patch"), None),
    )
    out_specs = (P(("visit", "patch"), None, None), P("patch", None, None))
    return jax.shard_map(local, mesh=mesh, in_specs=in_specs, out_specs=out_specs, check_vma=False)
```

```python
import functools
import jax
import jax.numpy as jnp
from jax import lax
from jax.experimental import pallas as pl
from jax.experimental.pallas import tpu as pltpu
from jax.sharding import PartitionSpec as P

GRAIN = 16


def flip(number, other, size):
    result, bit = 0, 1
    while bit < size:
        mine, its = lax.rem(lax.div(number, bit), 2), other // bit % 2 if isinstance(other, int) else lax.rem(lax.div(other, bit), 2)
        result = result + bit * (mine + its - 2 * mine * its)
        bit *= 2
    return result


def loop(low, high, body):
    if high - low <= 4:
        for i in range(low, high):
            body(i)
    else:
        lax.fori_loop(low, high, lambda i, _: (body(i), 0)[1], 0)


def coadd_kernel(chips, visits, routes_far, weights_far, tiles, out, routes, weights, tbuf, mix, give, keep, half, chip_sum, inbox, mine,
                 lane_sum, lane_in, tot, tot_core, tot_chip, tot_plane, tot_lane,
                 small_s, load_s, core_s, core_r, chip_s, chip_r, lane_s, lane_r, back_s, back_r, fan_s, fan_r,
                 pair_s, pair_r, totc_s, totc_r, totp_s, totp_r, totz_s, totz_r):
    v = lax.axis_index("visit")
    p = lax.axis_index("patch")
    k, c = lax.div(p, 2), lax.rem(p, 2)
    patches = 2 * chips
    count, side, _ = tiles.shape
    rows = side // visits
    steps = [visits - 1 - i for i in range(visits)]
    order = [flip(v, o, visits) for o in steps]
    sibling = (v, 2 * k + 1 - c)

    def span(r):
        return pl.ds(pl.multiple_of(r * rows, rows), rows)

    def chip_at(o):
        return flip(k, o, chips)

    def plane_at(o):
        return (v, 2 * chip_at(o) + c)

    def visit_at(o):
        return flip(v, o, visits)

    def remote(src, dst, send, recv, device):
        return pltpu.make_async_remote_copy(
            src_ref=src, dst_ref=dst, send_sem=send, recv_sem=recv,
            device_id=device, device_id_type=pl.DeviceIdType.MESH)

    def load(i):
        piece = span(order[i])
        return pltpu.make_async_copy(tiles.at[:, piece], tbuf.at[:, piece], load_s.at[i])

    def core_copy(i):
        piece = span(order[i])
        return remote(give.at[:, piece], half.at[:, piece], core_s.at[i], core_r.at[i], sibling)

    def chip_copy(o, i):
        piece = span(order[i])
        return remote(chip_sum.at[o - 1, piece], inbox.at[o - 1, piece], chip_s.at[o - 1, i], chip_r.at[o - 1, i], plane_at(o))

    def lane_copy(o):
        return remote(lane_sum.at[o - 1], lane_in.at[o - 1], lane_s.at[o - 1], lane_r.at[o - 1], (visit_at(o), p))

    def back_copy(o, r):
        piece = out.at[k, c, span(r)]
        return remote(piece, piece, back_s.at[o - 1], back_r.at[o - 1], (visit_at(o), p))

    def fan_copy(o, i, chip):
        piece = out.at[chip, c, span(order[i])]
        return remote(piece, piece, fan_s.at[o - 1, i], fan_r.at[o - 1, i], plane_at(o))

    def pair_copy(i, core):
        piece = out.at[:, core, span(order[i])]
        return remote(piece, piece, pair_s.at[i], pair_r.at[i], sibling)

    def tot_core_copy():
        return remote(tot, tot_core, totc_s, totc_r, sibling)

    def tot_plane_copy(o):
        return remote(tot_chip, tot_plane.at[o - 1], totp_s.at[o - 1], totp_r.at[o - 1], plane_at(o))

    def tot_lane_copy(o):
        return remote(tot_core, tot_lane.at[o - 1], totz_s.at[o - 1], totz_r.at[o - 1], (visit_at(o), p))

    barrier = pltpu.get_barrier_semaphore()

    def greet(device):
        pl.semaphore_signal(barrier, inc=1, device_id=device, device_id_type=pl.DeviceIdType.MESH)

    small = [pltpu.make_async_copy(routes_far, routes, small_s.at[0]),
             pltpu.make_async_copy(weights_far, weights, small_s.at[1])]
    for copy in small:
        copy.start()
    for i in range(visits):
        load(i).start()
    greet(sibling)
    loop(1, chips, lambda o: greet(plane_at(o)))
    loop(1, visits, lambda o: greet((visit_at(o), p)))

    line = lax.broadcasted_iota(jnp.int32, (patches * GRAIN, count), 0)
    slot = lax.div(line, GRAIN)
    patch = jnp.where(slot < chips, 2 * slot + 1 - c, 2 * (slot - chips) + c)
    for copy in small:
        copy.wait()
    scales = weights[...].astype(jnp.float32)
    routed = jnp.where(routes[...] == patch, scales, 0.0).astype(jnp.bfloat16)
    grains = lax.div(lax.broadcasted_iota(jnp.int32, (count, count * GRAIN), 1), GRAIN)
    widen = (grains == lax.broadcasted_iota(jnp.int32, (count, count * GRAIN), 0)).astype(jnp.float32).astype(jnp.bfloat16)
    wide = jnp.dot(routed, widen, preferred_element_type=jnp.float32)
    same = lax.rem(lax.broadcasted_iota(jnp.int32, wide.shape, 0), GRAIN) == lax.rem(
        lax.broadcasted_iota(jnp.int32, wide.shape, 1), GRAIN)
    mix[...] = jnp.where(same, wide, 0.0).astype(jnp.bfloat16)
    named = jnp.where(routes[...] == lax.broadcasted_iota(jnp.int32, (patches, count), 0), scales, 0.0)
    tot[...] = jnp.dot(named.astype(jnp.bfloat16), jnp.ones((count, 128), jnp.bfloat16), preferred_element_type=jnp.float32)

    def sums(i):
        load(i).wait()
        for b in range(rows // GRAIN):
            piece = pl.ds(pl.multiple_of(order[i] * rows + b * GRAIN, GRAIN), GRAIN)
            got = jnp.dot(mix[...], tbuf[:, piece, :].reshape(count * GRAIN, side), preferred_element_type=jnp.float32)
            got = got.reshape(2, chips, GRAIN, side)
            give[:, piece, :] = got[0].astype(jnp.bfloat16)
            keep[:, piece, :] = got[1]

    def send_chips(i):
        core_copy(i).wait_recv()
        piece = span(order[i])

        def one(o):
            j = chip_at(o)
            chip_sum[o - 1, piece, :] = (keep[j, piece, :] + half[j, piece, :].astype(jnp.float32)).astype(jnp.bfloat16)
            chip_copy(o, i).start()

        loop(1, chips, one)

    def gather(i):
        piece = span(order[i])
        mine[...] = keep[k, piece, :] + half[k, piece, :].astype(jnp.float32)

        def one(o):
            chip_copy(o, i).wait_recv()
            mine[...] += inbox[o - 1, piece, :].astype(jnp.float32)

        loop(1, chips, one)

    sums(0)
    pl.semaphore_wait(barrier, 1 + chips - 1 + visits - 1)
    core_copy(0).start()
    tot_core_copy().start()
    for i in range(1, visits):
        sums(i)
        core_copy(i).start()
        send_chips(i - 1)
    tot_core_copy().wait()
    tot_chip[...] = tot[...] + tot_core[...]
    send_chips(visits - 1)
    loop(1, chips, lambda o: tot_plane_copy(o).start())

    for i in range(visits - 1):
        gather(i)
        lane_sum[steps[i] - 1] = mine[...].astype(jnp.bfloat16)
        lane_copy(steps[i]).start()
        if i == 0:
            tot_core[...] = tot_chip[...]

            def add_plane(o):
                tot_plane_copy(o).wait_recv()
                tot_core[...] += tot_plane[o - 1]

            loop(1, chips, add_plane)
            loop(1, visits, lambda o: tot_lane_copy(o).start())
    gather(visits - 1)
    tot[...] = tot_core[...]

    def add_lane(i):
        o = visits - 1 - i
        lane_copy(o).wait_recv()
        mine[...] += lane_in[o - 1].astype(jnp.float32)
        tot_lane_copy(o).wait_recv()
        tot[...] += tot_lane[o - 1]

    loop(0, visits - 1, add_lane)
    out[k, c, span(v), :] = (mine[...] / tot[pl.ds(p, 1), :][0:1, 0:1]).astype(jnp.bfloat16)

    def fan_out(i):
        loop(1, chips, lambda o: fan_copy(o, i, k).start())

    def forward(i):
        loop(1, chips, lambda o: fan_copy(o, i, chip_at(o)).wait_recv())
        pair_copy(i, c).start()

    loop(1, visits, lambda o: back_copy(o, v).start())
    fan_out(visits - 1)
    for i in range(visits - 2, -1, -1):
        back_copy(steps[i], order[i]).wait_recv()
        fan_out(i)
        forward(i + 1)
    forward(0)

    for i in range(visits - 1, -1, -1):
        pair_copy(i, 1 - c).wait_recv()

    def finish(i):
        core_copy(i).wait_send()
        pair_copy(i, c).wait_send()

        def peer(o):
            chip_copy(o, i).wait_send()
            fan_copy(o, i, k).wait_send()

        loop(1, chips, peer)

    for i in range(visits):
        finish(i)

    def finish_visit(o):
        lane_copy(o).wait_send()
        back_copy(o, v).wait_send()
        tot_lane_copy(o).wait_send()

    loop(1, visits, finish_visit)
    loop(1, chips, lambda o: tot_plane_copy(o).wait_send())


def coadds(tiles, weights, routes, patches, visits):
    count, side, _ = tiles.shape
    chips = patches // 2
    rows = side // visits
    dma = pltpu.SemaphoreType.DMA
    block = pl.BlockSpec(memory_space=pltpu.VMEM)
    far = pl.BlockSpec(memory_space=pltpu.HBM)
    lane = max(visits - 1, 1)
    peer = max(chips - 1, 1)
    bf16, f32 = jnp.bfloat16, jnp.float32
    return pl.pallas_call(
        functools.partial(coadd_kernel, chips, visits),
        in_specs=[far, far, far],
        out_specs=block,
        out_shape=jax.ShapeDtypeStruct((chips, 2, side, side), bf16),
        scratch_shapes=[
            pltpu.VMEM(routes.shape, routes.dtype),
            pltpu.VMEM(weights.shape, weights.dtype),
            pltpu.VMEM((count, side, side), bf16),
            pltpu.VMEM((patches * GRAIN, count * GRAIN), bf16),
            pltpu.VMEM((chips, side, side), bf16),
            pltpu.VMEM((chips, side, side), f32),
            pltpu.VMEM((chips, side, side), bf16),
            pltpu.VMEM((peer, side, side), bf16),
            pltpu.VMEM((peer, side, side), bf16),
            pltpu.VMEM((rows, side), f32),
            pltpu.VMEM((lane, rows, side), bf16),
            pltpu.VMEM((lane, rows, side), bf16),
            pltpu.VMEM((patches, 128), f32),
            pltpu.VMEM((patches, 128), f32),
            pltpu.VMEM((patches, 128), f32),
            pltpu.VMEM((peer, patches, 128), f32),
            pltpu.VMEM((lane, patches, 128), f32),
            dma((2,)), dma((visits,)), dma((visits,)), dma((visits,)), dma((peer, visits)), dma((peer, visits)),
            dma((lane,)), dma((lane,)), dma((lane,)), dma((lane,)), dma((peer, visits)), dma((peer, visits)),
            dma((visits,)), dma((visits,)), dma, dma, dma((peer,)), dma((peer,)), dma((lane,)), dma((lane,)),
        ],
        compiler_params=pltpu.CompilerParams(collective_id=0, has_side_effects=True, vmem_limit_bytes=40 << 20),
        name="coadds",
    )(*(pltpu.with_memory_space_constraint(x, pltpu.HBM) for x in (routes, weights, tiles)))


def band(row):
    half = 128
    ring = pltpu.roll(jnp.broadcast_to(row, (half, half)), 0, 1, stride=1, stride_axis=0)
    gap = lax.broadcasted_iota(jnp.int32, (half, half), 1) - lax.broadcasted_iota(jnp.int32, (half, half), 0)
    zero = jnp.zeros_like(ring)
    near = jnp.where((gap < 64) & (gap > -64), ring, zero).astype(jnp.bfloat16)
    upper = jnp.where(gap <= -64, ring, zero).astype(jnp.bfloat16)
    lower = jnp.where(gap >= 64, ring, zero).astype(jnp.bfloat16)
    return jnp.concatenate(
        [jnp.concatenate([near, upper], axis=1), jnp.concatenate([lower, near], axis=1)], axis=0
    )


def match_kernel(kernel, routes, taps, tiles, coadd, out, own, rings):
    step = pl.program_id(0)
    group = tiles.shape[0]

    @pl.when(step == 0)
    def _():
        tap = lax.broadcasted_iota(jnp.int32, (kernel, 128), 0)
        lane = lax.broadcasted_iota(jnp.int32, (kernel, 128), 1)
        reach = kernel // 2
        gap = jnp.where(lane >= 64, lane - 128, lane)
        for side, hot in enumerate((tap == reach + gap, tap == reach - gap)):
            rings[side] = lax.dot_general(
                taps[:, side, :], hot.astype(jnp.float32).astype(jnp.bfloat16), (((0,), (0,)), ((), ())),
                preferred_element_type=jnp.float32)
        own[0] = coadd[lax.axis_index("patch")]

    places = [step * group + g for g in range(group)]
    row_passes = [
        jnp.dot(
            band(rings[0, pl.ds(place, 1), :]), coadd[routes[place]], preferred_element_type=jnp.float32
        ).astype(jnp.bfloat16)
        for place in places
    ]
    for g, place in enumerate(places):
        template = jnp.dot(
            row_passes[g], band(rings[1, pl.ds(place, 1), :]), preferred_element_type=jnp.float32
        ).astype(jnp.bfloat16)
        out[g] = (tiles[g].astype(jnp.float32) - template.astype(jnp.float32)).astype(out.dtype)


def subtract(tiles, taps, routes, coadd, group):
    count, side, _ = tiles.shape
    kernel = taps.shape[2]
    flat = taps.transpose(2, 1, 0)
    return pl.pallas_call(
        functools.partial(match_kernel, kernel),
        grid_spec=pltpu.PrefetchScalarGridSpec(
            num_scalar_prefetch=1,
            grid=(count // group,),
            in_specs=[
                pl.BlockSpec(flat.shape, lambda i, *_: (0, 0, 0)),
                pl.BlockSpec((group, side, side), lambda i, *_: (i, 0, 0)),
                pl.BlockSpec(coadd.shape, lambda i, *_: (0, 0, 0)),
            ],
            out_specs=[
                pl.BlockSpec((group, side, side), lambda i, *_: (i, 0, 0)),
                pl.BlockSpec((1, side, side), lambda i, *_: (0, 0, 0)),
            ],
            scratch_shapes=[pltpu.VMEM((2, count, 128), jnp.float32)],
        ),
        out_shape=[
            jax.ShapeDtypeStruct(tiles.shape, jnp.bfloat16),
            jax.ShapeDtypeStruct((1, side, side), jnp.bfloat16),
        ],
        compiler_params=pltpu.CompilerParams(vmem_limit_bytes=24 << 20),
        name="subtract",
    )(routes, flat, tiles, coadd)


def local(warped_tiles, tile_weights, kernel_taps, patch_routes):
    patches = lax.axis_size("patch")
    side = warped_tiles.shape[1]
    coadd = coadds(warped_tiles, tile_weights[None, :], patch_routes.T, patches, lax.axis_size("visit"))
    return tuple(subtract(warped_tiles, kernel_taps, patch_routes[:, 0], coadd.reshape(patches, side, side), 16))


def solution(mesh):
    in_specs = (
        P(("visit", "patch"), None, None),
        P(("visit", "patch")),
        P(("visit", "patch"), None, None),
        P(("visit", "patch"), None),
    )
    out_specs = (P(("visit", "patch"), None, None), P("patch", None, None))
    return jax.shard_map(local, mesh=mesh, in_specs=in_specs, out_specs=out_specs, check_vma=False)
```

```python
import functools
import jax
import jax.numpy as jnp
from jax import lax
from jax.experimental import pallas as pl
from jax.experimental.pallas import tpu as pltpu
from jax.sharding import PartitionSpec as P

GRAIN = 16
PARTS = 1


def flip(number, other, size):
    result, bit = 0, 1
    while bit < size:
        mine, its = lax.rem(lax.div(number, bit), 2), other // bit % 2 if isinstance(other, int) else lax.rem(lax.div(other, bit), 2)
        result = result + bit * (mine + its - 2 * mine * its)
        bit *= 2
    return result


def loop(low, high, body):
    if high - low <= 4:
        for i in range(low, high):
            body(i)
    else:
        lax.fori_loop(low, high, lambda i, _: (body(i), 0)[1], 0)


def coadd_kernel(chips, visits, parts, routes_far, weights_far, tiles, out, routes, weights, tbuf, mix, give, keep, half, chip_sum, inbox, mine, held,
                 lane_sum, lane_in, tot, tot_core, tot_chip, tot_plane, tot_lane,
                 small_s, load_s, core_s, core_r, chip_s, chip_r, lane_s, lane_r, back_s, back_r, fan_s, fan_r,
                 pair_s, pair_r, totc_s, totc_r, totp_s, totp_r, totz_s, totz_r):
    v = lax.axis_index("visit")
    p = lax.axis_index("patch")
    k, c = lax.div(p, 2), lax.rem(p, 2)
    patches = 2 * chips
    count, side, _ = tiles.shape
    rows = side // visits
    units = parts * visits
    sub = rows // parts
    steps = [visits - 1 - n % visits for n in range(units)]
    others = [flip(v, o, visits) for o in range(visits)]
    firsts = [others[steps[n]] * rows + n // visits * sub for n in range(units)]
    sibling = (v, 2 * k + 1 - c)

    def span(n):
        return pl.ds(pl.multiple_of(firsts[n], sub), sub)

    known = {}

    def chip_at(o):
        if not isinstance(o, int):
            return flip(k, o, chips)
        if o not in known:
            known[o] = flip(k, o, chips)
        return known[o]

    def plane_at(o):
        return (v, 2 * chip_at(o) + c)

    def visit_at(o):
        return others[o] if isinstance(o, int) else flip(v, o, visits)

    def remote(src, dst, send, recv, device):
        return pltpu.make_async_remote_copy(
            src_ref=src, dst_ref=dst, send_sem=send, recv_sem=recv,
            device_id=device, device_id_type=pl.DeviceIdType.MESH)

    def load(i):
        piece = span(i)
        return pltpu.make_async_copy(tiles.at[:, piece], tbuf.at[:, piece], load_s.at[i])

    def core_copy(i):
        piece = span(i)
        return remote(give.at[:, piece], half.at[:, piece], core_s.at[i], core_r.at[i], sibling)

    def chip_copy(o, i):
        piece = span(i)
        return remote(chip_sum.at[o - 1, piece], inbox.at[o - 1, piece], chip_s.at[o - 1, i], chip_r.at[o - 1, i], plane_at(o))

    def lane_copy(s, o):
        return remote(lane_sum.at[s, o - 1], lane_in.at[s, o - 1], lane_s.at[s, o - 1], lane_r.at[s, o - 1], (visit_at(o), p))

    def own_unit(s):
        return s * visits + visits - 1

    def back_copy(s, o, n):
        piece = out.at[k, c, span(n)]
        return remote(piece, piece, back_s.at[s, o - 1], back_r.at[s, o - 1], (visit_at(o), p))

    def fan_copy(o, i, chip):
        piece = out.at[chip, c, span(i)]
        return remote(piece, piece, fan_s.at[o - 1, i], fan_r.at[o - 1, i], plane_at(o))

    def pair_copy(i, core):
        piece = out.at[:, core, span(i)]
        return remote(piece, piece, pair_s.at[i], pair_r.at[i], sibling)

    def tot_core_copy():
        return remote(tot, tot_core, totc_s, totc_r, sibling)

    def tot_plane_copy(o):
        return remote(tot_chip, tot_plane.at[o - 1], totp_s.at[o - 1], totp_r.at[o - 1], plane_at(o))

    def tot_lane_copy(o):
        return remote(tot_core, tot_lane.at[o - 1], totz_s.at[o - 1], totz_r.at[o - 1], (visit_at(o), p))

    barrier = pltpu.get_barrier_semaphore()

    def greet(device):
        pl.semaphore_signal(barrier, inc=1, device_id=device, device_id_type=pl.DeviceIdType.MESH)

    small = [pltpu.make_async_copy(routes_far, routes, small_s.at[0]),
             pltpu.make_async_copy(weights_far, weights, small_s.at[1])]
    for copy in small:
        copy.start()
    for o in range(1, chips if chips <= 4 else 1):
        chip_at(o)
    for i in range(units):
        load(i).start()
    greet(sibling)
    loop(1, chips, lambda o: greet(plane_at(o)))
    loop(1, visits, lambda o: greet((visit_at(o), p)))

    line = lax.broadcasted_iota(jnp.int32, (patches * GRAIN, count), 0)
    slot = lax.div(line, GRAIN)
    patch = jnp.where(slot < chips, 2 * slot + 1 - c, 2 * (slot - chips) + c)
    for copy in small:
        copy.wait()
    scales = weights[...].astype(jnp.float32)
    routed = jnp.where(routes[...] == patch, scales, 0.0).astype(jnp.bfloat16)
    grains = lax.div(lax.broadcasted_iota(jnp.int32, (count, count * GRAIN), 1), GRAIN)
    widen = (grains == lax.broadcasted_iota(jnp.int32, (count, count * GRAIN), 0)).astype(jnp.float32).astype(jnp.bfloat16)
    wide = jnp.dot(routed, widen, preferred_element_type=jnp.float32)
    same = lax.rem(lax.broadcasted_iota(jnp.int32, wide.shape, 0), GRAIN) == lax.rem(
        lax.broadcasted_iota(jnp.int32, wide.shape, 1), GRAIN)
    mix[...] = jnp.where(same, wide, 0.0).astype(jnp.bfloat16)
    named = jnp.where(routes[...] == lax.broadcasted_iota(jnp.int32, (patches, count), 0), scales, 0.0)
    tot[...] = jnp.dot(named.astype(jnp.bfloat16), jnp.ones((count, 128), jnp.bfloat16), preferred_element_type=jnp.float32)

    def sums(i):
        load(i).wait()
        for b in range(sub // GRAIN):
            piece = pl.ds(pl.multiple_of(firsts[i] + b * GRAIN, GRAIN), GRAIN)
            got = jnp.dot(mix[...], tbuf[:, piece, :].reshape(count * GRAIN, side), preferred_element_type=jnp.float32)
            got = got.reshape(2, chips, GRAIN, side)
            give[:, piece, :] = got[0].astype(jnp.bfloat16)
            keep[:, piece, :] = got[1]

    def send_chips(i):
        core_copy(i).wait_recv()
        piece = span(i)

        def one(o):
            j = chip_at(o)
            chip_sum[o - 1, piece, :] = (keep[j, piece, :] + half[j, piece, :].astype(jnp.float32)).astype(jnp.bfloat16)
            chip_copy(o, i).start()

        loop(1, chips, one)

    def gather(i):
        piece = span(i)
        mine[...] = keep[k, piece, :] + half[k, piece, :].astype(jnp.float32)

        def one(o):
            chip_copy(o, i).wait_recv()
            mine[...] += inbox[o - 1, piece, :].astype(jnp.float32)

        loop(1, chips, one)

    sums(0)
    pl.semaphore_wait(barrier, 1 + chips - 1 + visits - 1)
    core_copy(0).start()
    tot_core_copy().start()
    for i in range(1, units):
        sums(i)
        core_copy(i).start()
        send_chips(i - 1)
    tot_core_copy().wait()
    tot_chip[...] = tot[...] + tot_core[...]
    send_chips(units - 1)
    loop(1, chips, lambda o: tot_plane_copy(o).start())

    def total_of_plane():
        tot_core[...] = tot_chip[...]

        def add_plane(o):
            tot_plane_copy(o).wait_recv()
            tot_core[...] += tot_plane[o - 1]

        loop(1, chips, add_plane)
        loop(1, visits, lambda o: tot_lane_copy(o).start())

    def total_of_lane():
        tot[...] = tot_core[...]

        def add_lane(o):
            tot_lane_copy(o).wait_recv()
            tot[...] += tot_lane[o - 1]

        loop(1, visits, add_lane)

    for n in range(units):
        s = n // visits
        gather(n)
        if steps[n]:
            lane_sum[s, steps[n] - 1] = mine[...].astype(jnp.bfloat16)
            lane_copy(s, steps[n]).start()
        else:
            held[s] = mine[...]
        if n == 0:
            total_of_plane()

    def fan_out(n):
        loop(1, chips, lambda o: fan_copy(o, n, k).start())

    def forward(n):
        loop(1, chips, lambda o: fan_copy(o, n, chip_at(o)).wait_recv())
        pair_copy(n, c).start()

    for s in range(parts):
        for o in range(visits - 1, 0, -1):
            lane_copy(s, o).wait_recv()
            held[s] += lane_in[s, o - 1].astype(jnp.float32)
        if s == 0:
            total_of_lane()
        own = own_unit(s)
        out[k, c, span(own), :] = (held[s] / tot[pl.ds(p, 1), :][0:1, 0:1]).astype(jnp.bfloat16)
        for o in range(1, visits):
            back_copy(s, o, own).start()
        fan_out(own)

    for s in range(parts):
        for o in range(1, visits):
            n = own_unit(s) - o
            back_copy(s, o, n).wait_recv()
            fan_out(n)
        forward(own_unit(s))
    for s in range(parts):
        for o in range(1, visits):
            forward(own_unit(s) - o)

    for n in range(units):
        pair_copy(n, 1 - c).wait_recv()

    for n in range(units):
        core_copy(n).wait_send()
        pair_copy(n, c).wait_send()

        def peer(o):
            chip_copy(o, n).wait_send()
            fan_copy(o, n, k).wait_send()

        loop(1, chips, peer)

    for s in range(parts):
        for o in range(1, visits):
            lane_copy(s, o).wait_send()
            back_copy(s, o, own_unit(s)).wait_send()
    loop(1, visits, lambda o: tot_lane_copy(o).wait_send())
    loop(1, chips, lambda o: tot_plane_copy(o).wait_send())


def coadds(tiles, weights, routes, patches, visits):
    count, side, _ = tiles.shape
    chips = patches // 2
    rows = side // visits
    parts = PARTS if rows % (PARTS * GRAIN) == 0 else 1
    units, sub = parts * visits, rows // parts
    dma = pltpu.SemaphoreType.DMA
    block = pl.BlockSpec(memory_space=pltpu.VMEM)
    far = pl.BlockSpec(memory_space=pltpu.HBM)
    lane = max(visits - 1, 1)
    peer = max(chips - 1, 1)
    bf16, f32 = jnp.bfloat16, jnp.float32
    return pl.pallas_call(
        functools.partial(coadd_kernel, chips, visits, parts),
        in_specs=[far, far, far],
        out_specs=block,
        out_shape=jax.ShapeDtypeStruct((chips, 2, side, side), bf16),
        scratch_shapes=[
            pltpu.VMEM(routes.shape, routes.dtype),
            pltpu.VMEM(weights.shape, weights.dtype),
            pltpu.VMEM((count, side, side), bf16),
            pltpu.VMEM((patches * GRAIN, count * GRAIN), bf16),
            pltpu.VMEM((chips, side, side), bf16),
            pltpu.VMEM((chips, side, side), f32),
            pltpu.VMEM((chips, side, side), bf16),
            pltpu.VMEM((peer, side, side), bf16),
            pltpu.VMEM((peer, side, side), bf16),
            pltpu.VMEM((sub, side), f32),
            pltpu.VMEM((parts, sub, side), f32),
            pltpu.VMEM((parts, lane, sub, side), bf16),
            pltpu.VMEM((parts, lane, sub, side), bf16),
            pltpu.VMEM((patches, 128), f32),
            pltpu.VMEM((patches, 128), f32),
            pltpu.VMEM((patches, 128), f32),
            pltpu.VMEM((peer, patches, 128), f32),
            pltpu.VMEM((lane, patches, 128), f32),
            dma((2,)), dma((units,)), dma((units,)), dma((units,)), dma((peer, units)), dma((peer, units)),
            dma((parts, lane)), dma((parts, lane)), dma((parts, lane)), dma((parts, lane)), dma((peer, units)), dma((peer, units)),
            dma((units,)), dma((units,)), dma, dma, dma((peer,)), dma((peer,)), dma((lane,)), dma((lane,)),
        ],
        compiler_params=pltpu.CompilerParams(collective_id=0, has_side_effects=True, vmem_limit_bytes=40 << 20),
        name="coadds",
    )(*(pltpu.with_memory_space_constraint(x, pltpu.HBM) for x in (routes, weights, tiles)))


def band(row):
    half = 128
    ring = pltpu.roll(jnp.broadcast_to(row, (half, half)), 0, 1, stride=1, stride_axis=0)
    gap = lax.broadcasted_iota(jnp.int32, (half, half), 1) - lax.broadcasted_iota(jnp.int32, (half, half), 0)
    zero = jnp.zeros_like(ring)
    near = jnp.where((gap < 64) & (gap > -64), ring, zero).astype(jnp.bfloat16)
    upper = jnp.where(gap <= -64, ring, zero).astype(jnp.bfloat16)
    lower = jnp.where(gap >= 64, ring, zero).astype(jnp.bfloat16)
    return jnp.concatenate(
        [jnp.concatenate([near, upper], axis=1), jnp.concatenate([lower, near], axis=1)], axis=0
    )


def match_kernel(kernel, group, routes, taps, tiles, coadd, out, own, rings, ready, sent, own_sent):
    count, side, _ = tiles.shape
    tap = lax.broadcasted_iota(jnp.int32, (kernel, 128), 0)
    lane = lax.broadcasted_iota(jnp.int32, (kernel, 128), 1)
    reach = kernel // 2
    gap = jnp.where(lane >= 64, lane - 128, lane)
    mine = pltpu.make_async_copy(coadd.at[lax.axis_index("patch")], own.at[0], own_sent)
    mine.start()
    for side_, hot in enumerate((tap == reach + gap, tap == reach - gap)):
        rings[side_] = lax.dot_general(
            taps[:, side_, :], hot.astype(jnp.float32).astype(jnp.bfloat16), (((0,), (0,)), ((), ())),
            preferred_element_type=jnp.float32)

    def send(g):
        piece = pl.ds(g * group, group)
        return pltpu.make_async_copy(ready.at[piece], out.at[piece], sent.at[g])

    def rows(g):
        return [
            jnp.dot(band(rings[0, place : place + 1, :]), coadd[routes[place]],
                    preferred_element_type=jnp.float32).astype(jnp.bfloat16)
            for place in range(g * group, (g + 1) * group)]

    passes = rows(0)
    for g in range(count // group):
        later = rows(g + 1) if False and g + 1 < count // group else None
        for i in range(group):
            place = g * group + i
            template = jnp.dot(passes[i], band(rings[1, place : place + 1, :]),
                               preferred_element_type=jnp.float32).astype(jnp.bfloat16)
            ready[place] = (tiles[place].astype(jnp.float32) - template.astype(jnp.float32)).astype(jnp.bfloat16)
        send(g).start()
        if g + 1 < count // group:
            passes = later if False else rows(g + 1)
    for g in range(count // group):
        send(g).wait()
    mine.wait()


def subtract(tiles, taps, routes, coadd, group):
    count, side, _ = tiles.shape
    kernel = taps.shape[2]
    block = pl.BlockSpec(memory_space=pltpu.VMEM)
    return pl.pallas_call(
        functools.partial(match_kernel, kernel, group),
        in_specs=[pl.BlockSpec(memory_space=pltpu.SMEM), block, block, block],
        out_specs=[pl.BlockSpec(memory_space=pltpu.HBM)] * 2,
        out_shape=[
            pltpu.HBM(tiles.shape, jnp.bfloat16),
            pltpu.HBM((1, side, side), jnp.bfloat16),
        ],
        scratch_shapes=[
            pltpu.VMEM((2, count, 128), jnp.float32),
            pltpu.VMEM(tiles.shape, jnp.bfloat16),
            pltpu.SemaphoreType.DMA((count // group,)),
            pltpu.SemaphoreType.DMA,
        ],
        compiler_params=pltpu.CompilerParams(vmem_limit_bytes=24 << 20),
        name="subtract",
    )(routes, taps.transpose(2, 1, 0), tiles, coadd)


def local(warped_tiles, tile_weights, kernel_taps, patch_routes):
    patches = lax.axis_size("patch")
    side = warped_tiles.shape[1]
    coadd = coadds(warped_tiles, tile_weights[None, :], patch_routes.T, patches, lax.axis_size("visit"))
    return tuple(subtract(warped_tiles, kernel_taps, patch_routes[:, 0], coadd.reshape(patches, side, side), 4))


def solution(mesh):
    in_specs = (
        P(("visit", "patch"), None, None),
        P(("visit", "patch")),
        P(("visit", "patch"), None, None),
        P(("visit", "patch"), None),
    )
    out_specs = (P(("visit", "patch"), None, None), P("patch", None, None))
    return jax.shard_map(local, mesh=mesh, in_specs=in_specs, out_specs=out_specs, check_vma=False)
```

```python
import functools
import jax
import jax.numpy as jnp
from jax import lax
from jax.experimental import pallas as pl
from jax.experimental.pallas import tpu as pltpu
from jax.sharding import PartitionSpec as P

GRAIN = 16
PARTS = 1
WINDOW = 3


def flip(number, other, size):
    result, bit = 0, 1
    while bit < size:
        mine, its = lax.rem(lax.div(number, bit), 2), other // bit % 2 if isinstance(other, int) else lax.rem(lax.div(other, bit), 2)
        result = result + bit * (mine + its - 2 * mine * its)
        bit *= 2
    return result


def loop(low, high, body):
    if high - low <= 4:
        for i in range(low, high):
            body(i)
    else:
        lax.fori_loop(low, high, lambda i, _: (body(i), 0)[1], 0)


def coadd_kernel(chips, visits, parts, routes_far, weights_far, tiles, out, routes, weights, tbuf, mix, give, keep, half, chip_sum, inbox, mine, held,
                 lane_sum, lane_in, tot, tot_core, tot_chip, tot_plane, tot_lane,
                 small_s, load_s, core_s, core_r, chip_s, chip_r, lane_s, lane_r, back_s, back_r, fan_s, fan_r,
                 pair_s, pair_r, totc_s, totc_r, totp_s, totp_r, totz_s, totz_r):
    v = lax.axis_index("visit")
    p = lax.axis_index("patch")
    k, c = lax.div(p, 2), lax.rem(p, 2)
    patches = 2 * chips
    count, side, _ = tiles.shape
    rows = side // visits
    units = parts * visits
    sub = rows // parts
    steps = [visits - 1 - n % visits for n in range(units)]
    others = [flip(v, o, visits) for o in range(visits)]
    firsts = [others[steps[n]] * rows + n // visits * sub for n in range(units)]
    sibling = (v, 2 * k + 1 - c)

    def span(n):
        return pl.ds(pl.multiple_of(firsts[n], sub), sub)

    known = {}

    def chip_at(o):
        if not isinstance(o, int):
            return flip(k, o, chips)
        if o not in known:
            known[o] = flip(k, o, chips)
        return known[o]

    def plane_at(o):
        return (v, 2 * chip_at(o) + c)

    def visit_at(o):
        return others[o] if isinstance(o, int) else flip(v, o, visits)

    def remote(src, dst, send, recv, device):
        return pltpu.make_async_remote_copy(
            src_ref=src, dst_ref=dst, send_sem=send, recv_sem=recv,
            device_id=device, device_id_type=pl.DeviceIdType.MESH)

    def load(i):
        piece = span(i)
        return pltpu.make_async_copy(tiles.at[:, piece], tbuf.at[:, piece], load_s.at[i])

    def core_copy(i):
        piece = span(i)
        return remote(give.at[:, piece], half.at[:, piece], core_s.at[i], core_r.at[i], sibling)

    def chip_copy(o, i):
        piece = span(i)
        return remote(chip_sum.at[o - 1, piece], inbox.at[o - 1, piece], chip_s.at[o - 1, i], chip_r.at[o - 1, i], plane_at(o))

    def lane_copy(s, o):
        return remote(lane_sum.at[s, o - 1], lane_in.at[s, o - 1], lane_s.at[s, o - 1], lane_r.at[s, o - 1], (visit_at(o), p))

    def own_unit(s):
        return s * visits + visits - 1

    def back_copy(s, o, n):
        piece = out.at[k, c, span(n)]
        return remote(piece, piece, back_s.at[s, o - 1], back_r.at[s, o - 1], (visit_at(o), p))

    def fan_copy(o, i, chip):
        piece = out.at[chip, c, span(i)]
        return remote(piece, piece, fan_s.at[o - 1, i], fan_r.at[o - 1, i], plane_at(o))

    def pair_copy(i, core):
        piece = out.at[:, core, span(i)]
        return remote(piece, piece, pair_s.at[i], pair_r.at[i], sibling)

    def tot_core_copy():
        return remote(tot, tot_core, totc_s, totc_r, sibling)

    def tot_plane_copy(o):
        return remote(tot_chip, tot_plane.at[o - 1], totp_s.at[o - 1], totp_r.at[o - 1], plane_at(o))

    def tot_lane_copy(o):
        return remote(tot_core, tot_lane.at[o - 1], totz_s.at[o - 1], totz_r.at[o - 1], (visit_at(o), p))

    barrier = pltpu.get_barrier_semaphore()

    def greet(device):
        pl.semaphore_signal(barrier, inc=1, device_id=device, device_id_type=pl.DeviceIdType.MESH)

    small = [pltpu.make_async_copy(routes_far, routes, small_s.at[0]),
             pltpu.make_async_copy(weights_far, weights, small_s.at[1])]
    for copy in small:
        copy.start()
    for o in range(1, chips if chips <= 4 else 1):
        chip_at(o)
    for i in range(units):
        load(i).start()
    greet(sibling)
    loop(1, chips, lambda o: greet(plane_at(o)))
    loop(1, visits, lambda o: greet((visit_at(o), p)))

    line = lax.broadcasted_iota(jnp.int32, (patches * GRAIN, count), 0)
    slot = lax.div(line, GRAIN)
    patch = jnp.where(slot < chips, 2 * slot + 1 - c, 2 * (slot - chips) + c)
    for copy in small:
        copy.wait()
    scales = weights[...].astype(jnp.float32)
    routed = jnp.where(routes[...] == patch, scales, 0.0).astype(jnp.bfloat16)
    grains = lax.div(lax.broadcasted_iota(jnp.int32, (count, count * GRAIN), 1), GRAIN)
    widen = (grains == lax.broadcasted_iota(jnp.int32, (count, count * GRAIN), 0)).astype(jnp.float32).astype(jnp.bfloat16)
    wide = jnp.dot(routed, widen, preferred_element_type=jnp.float32)
    same = lax.rem(lax.broadcasted_iota(jnp.int32, wide.shape, 0), GRAIN) == lax.rem(
        lax.broadcasted_iota(jnp.int32, wide.shape, 1), GRAIN)
    mix[...] = jnp.where(same, wide, 0.0).astype(jnp.bfloat16)
    named = jnp.where(routes[...] == lax.broadcasted_iota(jnp.int32, (patches, count), 0), scales, 0.0)
    tot[...] = jnp.dot(named.astype(jnp.bfloat16), jnp.ones((count, 128), jnp.bfloat16), preferred_element_type=jnp.float32)

    def sums(i):
        load(i).wait()
        for b in range(sub // GRAIN):
            piece = pl.ds(pl.multiple_of(firsts[i] + b * GRAIN, GRAIN), GRAIN)
            got = jnp.dot(mix[...], tbuf[:, piece, :].reshape(count * GRAIN, side), preferred_element_type=jnp.float32)
            got = got.reshape(2, chips, GRAIN, side)
            give[:, piece, :] = got[0].astype(jnp.bfloat16)
            keep[:, piece, :] = got[1]

    def send_chips(i):
        core_copy(i).wait_recv()
        piece = span(i)

        def one(o):
            j = chip_at(o)
            chip_sum[o - 1, piece, :] = (keep[j, piece, :] + half[j, piece, :].astype(jnp.float32)).astype(jnp.bfloat16)
            chip_copy(o, i).start()

        loop(1, chips, one)

    def gather(i):
        piece = span(i)
        mine[...] = keep[k, piece, :] + half[k, piece, :].astype(jnp.float32)

        def one(o):
            chip_copy(o, i).wait_recv()
            mine[...] += inbox[o - 1, piece, :].astype(jnp.float32)

        loop(1, chips, one)

    sums(0)
    pl.semaphore_wait(barrier, 1 + chips - 1 + visits - 1)
    core_copy(0).start()
    tot_core_copy().start()
    for i in range(1, units):
        sums(i)
        core_copy(i).start()
        if i <= WINDOW:
            send_chips(i - 1)
    tot_core_copy().wait()
    tot_chip[...] = tot[...] + tot_core[...]
    if units <= WINDOW:
        send_chips(units - 1)
    loop(1, chips, lambda o: tot_plane_copy(o).start())

    def total_of_plane():
        tot_core[...] = tot_chip[...]

        def add_plane(o):
            tot_plane_copy(o).wait_recv()
            tot_core[...] += tot_plane[o - 1]

        loop(1, chips, add_plane)
        loop(1, visits, lambda o: tot_lane_copy(o).start())

    def total_of_lane():
        tot[...] = tot_core[...]

        def add_lane(o):
            tot_lane_copy(o).wait_recv()
            tot[...] += tot_lane[o - 1]

        loop(1, visits, add_lane)

    for n in range(units):
        s = n // visits
        gather(n)
        if steps[n]:
            lane_sum[s, steps[n] - 1] = mine[...].astype(jnp.bfloat16)
            lane_copy(s, steps[n]).start()
        else:
            held[s] = mine[...]
        if n + WINDOW < units:
            send_chips(n + WINDOW)
        if n == 0:
            total_of_plane()

    def fan_out(n):
        loop(1, chips, lambda o: fan_copy(o, n, k).start())

    def forward(n):
        loop(1, chips, lambda o: fan_copy(o, n, chip_at(o)).wait_recv())
        pair_copy(n, c).start()

    for s in range(parts):
        for o in range(visits - 1, 0, -1):
            lane_copy(s, o).wait_recv()
            held[s] += lane_in[s, o - 1].astype(jnp.float32)
        if s == 0:
            total_of_lane()
        own = own_unit(s)
        out[k, c, span(own), :] = (held[s] / tot[pl.ds(p, 1), :][0:1, 0:1]).astype(jnp.bfloat16)
        for o in range(1, visits):
            back_copy(s, o, own).start()
        fan_out(own)

    for s in range(parts):
        for o in range(1, visits):
            n = own_unit(s) - o
            back_copy(s, o, n).wait_recv()
            fan_out(n)
        forward(own_unit(s))
    for s in range(parts):
        for o in range(1, visits):
            forward(own_unit(s) - o)

    for n in range(units):
        pair_copy(n, 1 - c).wait_recv()

    for n in range(units):
        core_copy(n).wait_send()
        pair_copy(n, c).wait_send()

        def peer(o):
            chip_copy(o, n).wait_send()
            fan_copy(o, n, k).wait_send()

        loop(1, chips, peer)

    for s in range(parts):
        for o in range(1, visits):
            lane_copy(s, o).wait_send()
            back_copy(s, o, own_unit(s)).wait_send()
    loop(1, visits, lambda o: tot_lane_copy(o).wait_send())
    loop(1, chips, lambda o: tot_plane_copy(o).wait_send())


def coadds(tiles, weights, routes, patches, visits):
    count, side, _ = tiles.shape
    chips = patches // 2
    rows = side // visits
    parts = PARTS if rows % (PARTS * GRAIN) == 0 else 1
    units, sub = parts * visits, rows // parts
    dma = pltpu.SemaphoreType.DMA
    block = pl.BlockSpec(memory_space=pltpu.VMEM)
    far = pl.BlockSpec(memory_space=pltpu.HBM)
    lane = max(visits - 1, 1)
    peer = max(chips - 1, 1)
    bf16, f32 = jnp.bfloat16, jnp.float32
    return pl.pallas_call(
        functools.partial(coadd_kernel, chips, visits, parts),
        in_specs=[far, far, far],
        out_specs=block,
        out_shape=jax.ShapeDtypeStruct((chips, 2, side, side), bf16),
        scratch_shapes=[
            pltpu.VMEM(routes.shape, routes.dtype),
            pltpu.VMEM(weights.shape, weights.dtype),
            pltpu.VMEM((count, side, side), bf16),
            pltpu.VMEM((patches * GRAIN, count * GRAIN), bf16),
            pltpu.VMEM((chips, side, side), bf16),
            pltpu.VMEM((chips, side, side), f32),
            pltpu.VMEM((chips, side, side), bf16),
            pltpu.VMEM((peer, side, side), bf16),
            pltpu.VMEM((peer, side, side), bf16),
            pltpu.VMEM((sub, side), f32),
            pltpu.VMEM((parts, sub, side), f32),
            pltpu.VMEM((parts, lane, sub, side), bf16),
            pltpu.VMEM((parts, lane, sub, side), bf16),
            pltpu.VMEM((patches, 128), f32),
            pltpu.VMEM((patches, 128), f32),
            pltpu.VMEM((patches, 128), f32),
            pltpu.VMEM((peer, patches, 128), f32),
            pltpu.VMEM((lane, patches, 128), f32),
            dma((2,)), dma((units,)), dma((units,)), dma((units,)), dma((peer, units)), dma((peer, units)),
            dma((parts, lane)), dma((parts, lane)), dma((parts, lane)), dma((parts, lane)), dma((peer, units)), dma((peer, units)),
            dma((units,)), dma((units,)), dma, dma, dma((peer,)), dma((peer,)), dma((lane,)), dma((lane,)),
        ],
        compiler_params=pltpu.CompilerParams(collective_id=0, has_side_effects=True, vmem_limit_bytes=40 << 20),
        name="coadds",
    )(*(pltpu.with_memory_space_constraint(x, pltpu.HBM) for x in (routes, weights, tiles)))


def band(row):
    half = 128
    ring = pltpu.roll(jnp.broadcast_to(row, (half, half)), 0, 1, stride=1, stride_axis=0)
    gap = lax.broadcasted_iota(jnp.int32, (half, half), 1) - lax.broadcasted_iota(jnp.int32, (half, half), 0)
    zero = jnp.zeros_like(ring)
    near = jnp.where((gap < 64) & (gap > -64), ring, zero).astype(jnp.bfloat16)
    upper = jnp.where(gap <= -64, ring, zero).astype(jnp.bfloat16)
    lower = jnp.where(gap >= 64, ring, zero).astype(jnp.bfloat16)
    return jnp.concatenate(
        [jnp.concatenate([near, upper], axis=1), jnp.concatenate([lower, near], axis=1)], axis=0
    )


def match_kernel(kernel, group, routes, taps, tiles, coadd, out, own, rings, ready, sent, own_sent):
    count, side, _ = tiles.shape
    tap = lax.broadcasted_iota(jnp.int32, (kernel, 128), 0)
    lane = lax.broadcasted_iota(jnp.int32, (kernel, 128), 1)
    reach = kernel // 2
    gap = jnp.where(lane >= 64, lane - 128, lane)
    mine = pltpu.make_async_copy(coadd.at[lax.axis_index("patch")], own.at[0], own_sent)
    mine.start()
    for side_, hot in enumerate((tap == reach + gap, tap == reach - gap)):
        rings[side_] = lax.dot_general(
            taps[:, side_, :], hot.astype(jnp.float32).astype(jnp.bfloat16), (((0,), (0,)), ((), ())),
            preferred_element_type=jnp.float32)

    def send(g):
        piece = pl.ds(g * group, group)
        return pltpu.make_async_copy(ready.at[piece], out.at[piece], sent.at[g])

    def rows(g):
        return [
            jnp.dot(band(rings[0, place : place + 1, :]), coadd[routes[place]],
                    preferred_element_type=jnp.float32).astype(jnp.bfloat16)
            for place in range(g * group, (g + 1) * group)]

    passes = rows(0)
    for g in range(count // group):
        later = rows(g + 1) if False and g + 1 < count // group else None
        for i in range(group):
            place = g * group + i
            template = jnp.dot(passes[i], band(rings[1, place : place + 1, :]),
                               preferred_element_type=jnp.float32).astype(jnp.bfloat16)
            ready[place] = (tiles[place].astype(jnp.float32) - template.astype(jnp.float32)).astype(jnp.bfloat16)
        send(g).start()
        if g + 1 < count // group:
            passes = later if False else rows(g + 1)
    for g in range(count // group):
        send(g).wait()
    mine.wait()


def subtract(tiles, taps, routes, coadd, group):
    count, side, _ = tiles.shape
    kernel = taps.shape[2]
    block = pl.BlockSpec(memory_space=pltpu.VMEM)
    return pl.pallas_call(
        functools.partial(match_kernel, kernel, group),
        in_specs=[pl.BlockSpec(memory_space=pltpu.SMEM), block, block, block],
        out_specs=[pl.BlockSpec(memory_space=pltpu.HBM)] * 2,
        out_shape=[
            pltpu.HBM(tiles.shape, jnp.bfloat16),
            pltpu.HBM((1, side, side), jnp.bfloat16),
        ],
        scratch_shapes=[
            pltpu.VMEM((2, count, 128), jnp.float32),
            pltpu.VMEM(tiles.shape, jnp.bfloat16),
            pltpu.SemaphoreType.DMA((count // group,)),
            pltpu.SemaphoreType.DMA,
        ],
        compiler_params=pltpu.CompilerParams(vmem_limit_bytes=24 << 20),
        name="subtract",
    )(routes, taps.transpose(2, 1, 0), tiles, coadd)


def local(warped_tiles, tile_weights, kernel_taps, patch_routes):
    patches = lax.axis_size("patch")
    side = warped_tiles.shape[1]
    coadd = coadds(warped_tiles, tile_weights[None, :], patch_routes.T, patches, lax.axis_size("visit"))
    return tuple(subtract(warped_tiles, kernel_taps, patch_routes[:, 0], coadd.reshape(patches, side, side), 4))


def solution(mesh):
    in_specs = (
        P(("visit", "patch"), None, None),
        P(("visit", "patch")),
        P(("visit", "patch"), None, None),
        P(("visit", "patch"), None),
    )
    out_specs = (P(("visit", "patch"), None, None), P("patch", None, None))
    return jax.shard_map(local, mesh=mesh, in_specs=in_specs, out_specs=out_specs, check_vma=False)
```

```python
import functools
import jax
import jax.numpy as jnp
from jax import lax
from jax.experimental import pallas as pl
from jax.experimental.pallas import tpu as pltpu
from jax.sharding import PartitionSpec as P

GRAIN = 16


def flip(number, other, size):
    result, bit = 0, 1
    while bit < size:
        mine, its = lax.rem(lax.div(number, bit), 2), other // bit % 2 if isinstance(other, int) else lax.rem(lax.div(other, bit), 2)
        result = result + bit * (mine + its - 2 * mine * its)
        bit *= 2
    return result


def loop(low, high, body):
    if high - low <= 4:
        for i in range(low, high):
            body(i)
    else:
        lax.fori_loop(low, high, lambda i, _: (body(i), 0)[1], 0)


def coadd_kernel(chips, visits, routes_far, weights_far, tiles, out, routes, weights, tbuf, mix, give, keep, half, chip_sum, inbox, mine, near, near_in,
                 lane_sum, lane_in, tot, tot_core, tot_chip, tot_plane, tot_lane,
                 small_s, load_s, core_s, core_r, chip_s, chip_r, near_s, near_r, lane_s, lane_r, back_s, back_r, fan_s, fan_r,
                 pair_s, pair_r, totc_s, totc_r, totp_s, totp_r, totz_s, totz_r):
    v = lax.axis_index("visit")
    p = lax.axis_index("patch")
    k, c = lax.div(p, 2), lax.rem(p, 2)
    patches = 2 * chips
    count, side, _ = tiles.shape
    rows = side // visits
    steps = [1] + list(range(visits - 1, 1, -1)) + [0]
    others = [flip(v, o, visits) for o in range(visits)]
    units = range(visits)
    own = visits - 1
    sibling = (v, 2 * k + 1 - c)

    def span(n):
        return pl.ds(pl.multiple_of(others[steps[n]] * rows, rows), rows)

    known = {}

    def chip_at(o):
        if not isinstance(o, int):
            return flip(k, o, chips)
        if o not in known:
            known[o] = flip(k, o, chips)
        return known[o]

    def plane_at(o):
        return (v, 2 * chip_at(o) + c)

    def visit_at(o):
        return others[o] if isinstance(o, int) else flip(v, o, visits)

    def remote(src, dst, send, recv, device):
        return pltpu.make_async_remote_copy(
            src_ref=src, dst_ref=dst, send_sem=send, recv_sem=recv,
            device_id=device, device_id_type=pl.DeviceIdType.MESH)

    def load(i):
        piece = span(i)
        return pltpu.make_async_copy(tiles.at[:, piece], tbuf.at[:, piece], load_s.at[i])

    def core_copy(i):
        piece = span(i)
        return remote(give.at[:, piece], half.at[:, piece], core_s.at[i], core_r.at[i], sibling)

    def chip_copy(o, i):
        piece = span(i)
        return remote(chip_sum.at[o - 1, piece], inbox.at[o - 1, piece], chip_s.at[o - 1, i], chip_r.at[o - 1, i], plane_at(o))

    def near_copy():
        return remote(near, near_in, near_s, near_r, (others[1], p))

    def lane_copy(o):
        return remote(lane_sum.at[o - 2], lane_in.at[o - 2], lane_s.at[o - 2], lane_r.at[o - 2], (others[o], p))

    def back_copy(o, n):
        piece = out.at[k, c, span(n)]
        return remote(piece, piece, back_s.at[o - 1], back_r.at[o - 1], (others[o], p))

    def fan_copy(o, i, chip):
        piece = out.at[chip, c, span(i)]
        return remote(piece, piece, fan_s.at[o - 1, i], fan_r.at[o - 1, i], plane_at(o))

    def pair_copy(i, core):
        piece = out.at[:, core, span(i)]
        return remote(piece, piece, pair_s.at[i], pair_r.at[i], sibling)

    def tot_core_copy():
        return remote(tot, tot_core, totc_s, totc_r, sibling)

    def tot_plane_copy(o):
        return remote(tot_chip, tot_plane.at[o - 1], totp_s.at[o - 1], totp_r.at[o - 1], plane_at(o))

    def tot_lane_copy(o):
        return remote(tot_core, tot_lane.at[o - 1], totz_s.at[o - 1], totz_r.at[o - 1], (visit_at(o), p))

    barrier = pltpu.get_barrier_semaphore()

    def greet(device):
        pl.semaphore_signal(barrier, inc=1, device_id=device, device_id_type=pl.DeviceIdType.MESH)

    small = [pltpu.make_async_copy(routes_far, routes, small_s.at[0]),
             pltpu.make_async_copy(weights_far, weights, small_s.at[1])]
    for copy in small:
        copy.start()
    for o in range(1, chips if chips <= 4 else 1):
        chip_at(o)
    for i in units:
        load(i).start()
    greet(sibling)
    loop(1, chips, lambda o: greet(plane_at(o)))
    loop(1, visits, lambda o: greet((visit_at(o), p)))

    line = lax.broadcasted_iota(jnp.int32, (patches * GRAIN, count), 0)
    slot = lax.div(line, GRAIN)
    patch = jnp.where(slot < chips, 2 * slot + 1 - c, 2 * (slot - chips) + c)
    for copy in small:
        copy.wait()
    scales = weights[...].astype(jnp.float32)
    routed = jnp.where(routes[...] == patch, scales, 0.0).astype(jnp.bfloat16)
    grains = lax.div(lax.broadcasted_iota(jnp.int32, (count, count * GRAIN), 1), GRAIN)
    widen = (grains == lax.broadcasted_iota(jnp.int32, (count, count * GRAIN), 0)).astype(jnp.float32).astype(jnp.bfloat16)
    wide = jnp.dot(routed, widen, preferred_element_type=jnp.float32)
    same = lax.rem(lax.broadcasted_iota(jnp.int32, wide.shape, 0), GRAIN) == lax.rem(
        lax.broadcasted_iota(jnp.int32, wide.shape, 1), GRAIN)
    mix[...] = jnp.where(same, wide, 0.0).astype(jnp.bfloat16)
    named = jnp.where(routes[...] == lax.broadcasted_iota(jnp.int32, (patches, count), 0), scales, 0.0)
    tot[...] = jnp.dot(named.astype(jnp.bfloat16), jnp.ones((count, 128), jnp.bfloat16), preferred_element_type=jnp.float32)

    def sums(i):
        load(i).wait()
        for b in range(rows // GRAIN):
            piece = pl.ds(pl.multiple_of(others[steps[i]] * rows + b * GRAIN, GRAIN), GRAIN)
            got = jnp.dot(mix[...], tbuf[:, piece, :].reshape(count * GRAIN, side), preferred_element_type=jnp.float32)
            got = got.reshape(2, chips, GRAIN, side)
            give[:, piece, :] = got[0].astype(jnp.bfloat16)
            keep[:, piece, :] = got[1]

    def whole(i, j):
        total = keep[j, span(i), :] + half[j, span(i), :].astype(jnp.float32)
        return total + near_in[j].astype(jnp.float32) if i == own else total

    def send_near():
        core_copy(0).wait_recv()

        def one(j):
            near[j] = whole(0, j).astype(jnp.bfloat16)

        loop(0, chips, one)
        near_copy().start()

    def send_chips(i):
        core_copy(i).wait_recv()
        if i == own:
            near_copy().wait_recv()

        def one(o):
            chip_sum[o - 1, span(i), :] = whole(i, chip_at(o)).astype(jnp.bfloat16)
            chip_copy(o, i).start()

        loop(1, chips, one)

    def gather(i):
        piece = span(i)
        mine[...] = whole(i, k)

        def one(o):
            chip_copy(o, i).wait_recv()
            mine[...] += inbox[o - 1, piece, :].astype(jnp.float32)

        loop(1, chips, one)

    sums(0)
    pl.semaphore_wait(barrier, 1 + chips - 1 + visits - 1)
    core_copy(0).start()
    tot_core_copy().start()
    for i in range(1, visits):
        sums(i)
        core_copy(i).start()
        if i == 1:
            send_near()
        else:
            send_chips(i - 1)
    tot_core_copy().wait()
    tot_chip[...] = tot[...] + tot_core[...]
    loop(1, chips, lambda o: tot_plane_copy(o).start())

    def total_of_plane():
        tot_core[...] = tot_chip[...]

        def add_plane(o):
            tot_plane_copy(o).wait_recv()
            tot_core[...] += tot_plane[o - 1]

        loop(1, chips, add_plane)
        loop(1, visits, lambda o: tot_lane_copy(o).start())

    def total_of_lane():
        tot[...] = tot_core[...]

        def add_lane(o):
            tot_lane_copy(o).wait_recv()
            tot[...] += tot_lane[o - 1]

        loop(1, visits, add_lane)

    for n in range(1, own):
        if n == max(own - 1, 1):
            send_chips(own)
        gather(n)
        lane_sum[steps[n] - 2] = mine[...].astype(jnp.bfloat16)
        lane_copy(steps[n]).start()
        if n == 1:
            total_of_plane()
    gather(own)
    total_of_lane()
    for o in range(visits - 1, 1, -1):
        lane_copy(o).wait_recv()
        mine[...] += lane_in[o - 2].astype(jnp.float32)
    out[k, c, span(own), :] = (mine[...] / tot[pl.ds(p, 1), :][0:1, 0:1]).astype(jnp.bfloat16)

    def fan_out(n):
        loop(1, chips, lambda o: fan_copy(o, n, k).start())

    def forward(n):
        loop(1, chips, lambda o: fan_copy(o, n, chip_at(o)).wait_recv())
        pair_copy(n, c).start()

    back = [steps.index(o) for o in range(1, visits)]
    for o in range(1, visits):
        back_copy(o, own).start()
    fan_out(own)
    for o in range(1, visits):
        back_copy(o, back[o - 1]).wait_recv()
        fan_out(back[o - 1])
    for n in [own] + back:
        forward(n)

    for n in units:
        pair_copy(n, 1 - c).wait_recv()

    for n in units:
        core_copy(n).wait_send()
        pair_copy(n, c).wait_send()

        def peer(o):
            if n:
                chip_copy(o, n).wait_send()
            fan_copy(o, n, k).wait_send()

        loop(1, chips, peer)
    near_copy().wait_send()
    for o in range(1, visits):
        if o > 1:
            lane_copy(o).wait_send()
        back_copy(o, own).wait_send()
    loop(1, visits, lambda o: tot_lane_copy(o).wait_send())
    loop(1, chips, lambda o: tot_plane_copy(o).wait_send())


def coadds(tiles, weights, routes, patches, visits):
    count, side, _ = tiles.shape
    chips = patches // 2
    rows = side // visits
    dma = pltpu.SemaphoreType.DMA
    block = pl.BlockSpec(memory_space=pltpu.VMEM)
    far = pl.BlockSpec(memory_space=pltpu.HBM)
    lane = max(visits - 2, 1)
    peer = max(chips - 1, 1)
    bf16, f32 = jnp.bfloat16, jnp.float32
    return pl.pallas_call(
        functools.partial(coadd_kernel, chips, visits),
        in_specs=[far, far, far],
        out_specs=block,
        out_shape=jax.ShapeDtypeStruct((chips, 2, side, side), bf16),
        scratch_shapes=[
            pltpu.VMEM(routes.shape, routes.dtype),
            pltpu.VMEM(weights.shape, weights.dtype),
            pltpu.VMEM((count, side, side), bf16),
            pltpu.VMEM((patches * GRAIN, count * GRAIN), bf16),
            pltpu.VMEM((chips, side, side), bf16),
            pltpu.VMEM((chips, side, side), f32),
            pltpu.VMEM((chips, side, side), bf16),
            pltpu.VMEM((peer, side, side), bf16),
            pltpu.VMEM((peer, side, side), bf16),
            pltpu.VMEM((rows, side), f32),
            pltpu.VMEM((chips, rows, side), bf16),
            pltpu.VMEM((chips, rows, side), bf16),
            pltpu.VMEM((lane, rows, side), bf16),
            pltpu.VMEM((lane, rows, side), bf16),
            pltpu.VMEM((patches, 128), f32),
            pltpu.VMEM((patches, 128), f32),
            pltpu.VMEM((patches, 128), f32),
            pltpu.VMEM((peer, patches, 128), f32),
            pltpu.VMEM((visits - 1, patches, 128), f32),
            dma((2,)), dma((visits,)), dma((visits,)), dma((visits,)), dma((peer, visits)), dma((peer, visits)), dma, dma,
            dma((lane,)), dma((lane,)), dma((visits - 1,)), dma((visits - 1,)), dma((peer, visits)), dma((peer, visits)),
            dma((visits,)), dma((visits,)), dma, dma, dma((peer,)), dma((peer,)), dma((visits - 1,)), dma((visits - 1,)),
        ],
        compiler_params=pltpu.CompilerParams(collective_id=0, has_side_effects=True, vmem_limit_bytes=40 << 20),
        name="coadds",
    )(*(pltpu.with_memory_space_constraint(x, pltpu.HBM) for x in (routes, weights, tiles)))


def band(row):
    half = 128
    ring = pltpu.roll(jnp.broadcast_to(row, (half, half)), 0, 1, stride=1, stride_axis=0)
    gap = lax.broadcasted_iota(jnp.int32, (half, half), 1) - lax.broadcasted_iota(jnp.int32, (half, half), 0)
    zero = jnp.zeros_like(ring)
    near = jnp.where((gap < 64) & (gap > -64), ring, zero).astype(jnp.bfloat16)
    upper = jnp.where(gap <= -64, ring, zero).astype(jnp.bfloat16)
    lower = jnp.where(gap >= 64, ring, zero).astype(jnp.bfloat16)
    return jnp.concatenate(
        [jnp.concatenate([near, upper], axis=1), jnp.concatenate([lower, near], axis=1)], axis=0
    )


def match_kernel(kernel, group, routes, taps, tiles, coadd, out, own, rings, ready, sent, own_sent):
    count, side, _ = tiles.shape
    tap = lax.broadcasted_iota(jnp.int32, (kernel, 128), 0)
    lane = lax.broadcasted_iota(jnp.int32, (kernel, 128), 1)
    reach = kernel // 2
    gap = jnp.where(lane >= 64, lane - 128, lane)
    mine = pltpu.make_async_copy(coadd.at[lax.axis_index("patch")], own.at[0], own_sent)
    mine.start()
    for side_, hot in enumerate((tap == reach + gap, tap == reach - gap)):
        rings[side_] = lax.dot_general(
            taps[:, side_, :], hot.astype(jnp.float32).astype(jnp.bfloat16), (((0,), (0,)), ((), ())),
            preferred_element_type=jnp.float32)

    def send(g):
        piece = pl.ds(g * group, group)
        return pltpu.make_async_copy(ready.at[piece], out.at[piece], sent.at[g])

    def rows(g):
        return [
            jnp.dot(band(rings[0, place : place + 1, :]), coadd[routes[place]],
                    preferred_element_type=jnp.float32).astype(jnp.bfloat16)
            for place in range(g * group, (g + 1) * group)]

    passes = rows(0)
    for g in range(count // group):
        later = rows(g + 1) if False and g + 1 < count // group else None
        for i in range(group):
            place = g * group + i
            template = jnp.dot(passes[i], band(rings[1, place : place + 1, :]),
                               preferred_element_type=jnp.float32).astype(jnp.bfloat16)
            ready[place] = tiles[place] - template
        send(g).start()
        if g + 1 < count // group:
            passes = later if False else rows(g + 1)
    for g in range(count // group):
        send(g).wait()
    mine.wait()


def subtract(tiles, taps, routes, coadd, group):
    count, side, _ = tiles.shape
    kernel = taps.shape[2]
    block = pl.BlockSpec(memory_space=pltpu.VMEM)
    return pl.pallas_call(
        functools.partial(match_kernel, kernel, group),
        in_specs=[pl.BlockSpec(memory_space=pltpu.SMEM), block, block, block],
        out_specs=[pl.BlockSpec(memory_space=pltpu.HBM)] * 2,
        out_shape=[
            pltpu.HBM(tiles.shape, jnp.bfloat16),
            pltpu.HBM((1, side, side), jnp.bfloat16),
        ],
        scratch_shapes=[
            pltpu.VMEM((2, count, 128), jnp.float32),
            pltpu.VMEM(tiles.shape, jnp.bfloat16),
            pltpu.SemaphoreType.DMA((count // group,)),
            pltpu.SemaphoreType.DMA,
        ],
        compiler_params=pltpu.CompilerParams(vmem_limit_bytes=24 << 20),
        name="subtract",
    )(routes, taps.transpose(2, 1, 0), tiles, coadd)


def local(warped_tiles, tile_weights, kernel_taps, patch_routes):
    patches = lax.axis_size("patch")
    side = warped_tiles.shape[1]
    coadd = coadds(warped_tiles, tile_weights[None, :], patch_routes.T, patches, lax.axis_size("visit"))
    return tuple(subtract(warped_tiles, kernel_taps, patch_routes[:, 0], coadd.reshape(patches, side, side), 4))


def solution(mesh):
    in_specs = (
        P(("visit", "patch"), None, None),
        P(("visit", "patch")),
        P(("visit", "patch"), None, None),
        P(("visit", "patch"), None),
    )
    out_specs = (P(("visit", "patch"), None, None), P("patch", None, None))
    return jax.shard_map(local, mesh=mesh, in_specs=in_specs, out_specs=out_specs, check_vma=False)
```

```python
import functools
import jax
import jax.numpy as jnp
from jax import lax
from jax.experimental import pallas as pl
from jax.experimental.pallas import tpu as pltpu
from jax.sharding import PartitionSpec as P

GRAIN = 16


def flip(number, other, size):
    result, bit = 0, 1
    while bit < size:
        mine, its = lax.rem(lax.div(number, bit), 2), other // bit % 2 if isinstance(other, int) else lax.rem(lax.div(other, bit), 2)
        result = result + bit * (mine + its - 2 * mine * its)
        bit *= 2
    return result


def loop(low, high, body):
    if high - low <= 4:
        for i in range(low, high):
            body(i)
    else:
        lax.fori_loop(low, high, lambda i, _: (body(i), 0)[1], 0)


def coadd_kernel(chips, visits, routes_far, weights_far, tiles, out, routes, weights, tbuf, mix, give, keep, half, chip_sum, inbox, mine, near, near_in,
                 lane_sum, lane_in, tot, tot_core, tot_chip, tot_plane, tot_lane,
                 small_s, load_s, core_s, core_r, chip_s, chip_r, near_s, near_r, lane_s, lane_r, back_s, back_r, fan_s, fan_r,
                 pair_s, pair_r, totc_s, totc_r, totp_s, totp_r, totz_s, totz_r):
    v = lax.axis_index("visit")
    p = lax.axis_index("patch")
    k, c = lax.div(p, 2), lax.rem(p, 2)
    patches = 2 * chips
    count, side, _ = tiles.shape
    rows = side // visits
    steps = [visits - 1, 1] + list(range(visits - 2, 1, -1)) + [0]
    first = steps.index(1)
    farther = [n for n in range(visits) if steps[n] > 1]
    others = [flip(v, o, visits) for o in range(visits)]
    units = range(visits)
    own = visits - 1
    sibling = (v, 2 * k + 1 - c)

    def span(n):
        return pl.ds(pl.multiple_of(others[steps[n]] * rows, rows), rows)

    known = {}

    def chip_at(o):
        if not isinstance(o, int):
            return flip(k, o, chips)
        if o not in known:
            known[o] = flip(k, o, chips)
        return known[o]

    def plane_at(o):
        return (v, 2 * chip_at(o) + c)

    def visit_at(o):
        return others[o] if isinstance(o, int) else flip(v, o, visits)

    def remote(src, dst, send, recv, device):
        return pltpu.make_async_remote_copy(
            src_ref=src, dst_ref=dst, send_sem=send, recv_sem=recv,
            device_id=device, device_id_type=pl.DeviceIdType.MESH)

    def load(i):
        piece = span(i)
        return pltpu.make_async_copy(tiles.at[:, piece], tbuf.at[:, piece], load_s.at[i])

    def core_copy(i):
        piece = span(i)
        return remote(give.at[:, piece], half.at[:, piece], core_s.at[i], core_r.at[i], sibling)

    def chip_copy(o, i):
        piece = span(i)
        return remote(chip_sum.at[o - 1, piece], inbox.at[o - 1, piece], chip_s.at[o - 1, i], chip_r.at[o - 1, i], plane_at(o))

    def near_copy():
        return remote(near, near_in, near_s, near_r, (others[1], p))

    def lane_copy(o):
        return remote(lane_sum.at[o - 2], lane_in.at[o - 2], lane_s.at[o - 2], lane_r.at[o - 2], (others[o], p))

    def back_copy(o, n):
        piece = out.at[k, c, span(n)]
        return remote(piece, piece, back_s.at[o - 1], back_r.at[o - 1], (others[o], p))

    def fan_copy(o, i, chip):
        piece = out.at[chip, c, span(i)]
        return remote(piece, piece, fan_s.at[o - 1, i], fan_r.at[o - 1, i], plane_at(o))

    def pair_copy(i, core):
        piece = out.at[:, core, span(i)]
        return remote(piece, piece, pair_s.at[i], pair_r.at[i], sibling)

    def tot_core_copy():
        return remote(tot, tot_core, totc_s, totc_r, sibling)

    def tot_plane_copy(o):
        return remote(tot_chip, tot_plane.at[o - 1], totp_s.at[o - 1], totp_r.at[o - 1], plane_at(o))

    def tot_lane_copy(o):
        return remote(tot_core, tot_lane.at[o - 1], totz_s.at[o - 1], totz_r.at[o - 1], (visit_at(o), p))

    barrier = pltpu.get_barrier_semaphore()

    def greet(device):
        pl.semaphore_signal(barrier, inc=1, device_id=device, device_id_type=pl.DeviceIdType.MESH)

    small = [pltpu.make_async_copy(routes_far, routes, small_s.at[0]),
             pltpu.make_async_copy(weights_far, weights, small_s.at[1])]
    for copy in small:
        copy.start()
    for o in range(1, chips if chips <= 4 else 1):
        chip_at(o)
    for i in units:
        load(i).start()
    greet(sibling)
    loop(1, chips, lambda o: greet(plane_at(o)))
    loop(1, visits, lambda o: greet((visit_at(o), p)))

    slot = lax.shift_right_logical(lax.broadcasted_iota(jnp.int32, (patches * GRAIN, count), 0), 4)
    patch = jnp.where(slot < chips, 2 * slot + 1 - c, 2 * (slot - chips) + c)
    grain = (count, count * GRAIN)
    widen = (lax.shift_right_logical(lax.broadcasted_iota(jnp.int32, grain, 1), 4)
             == lax.broadcasted_iota(jnp.int32, grain, 0)).astype(jnp.float32).astype(jnp.bfloat16)
    grain = (GRAIN, count * GRAIN)
    same = lax.broadcasted_iota(jnp.int32, grain, 0) == (lax.broadcasted_iota(jnp.int32, grain, 1) & (GRAIN - 1))
    for copy in small:
        copy.wait()
    scales = weights[...].astype(jnp.float32)
    routed = jnp.where(routes[...] == patch, scales, 0.0).astype(jnp.bfloat16)
    wide = jnp.dot(routed, widen, preferred_element_type=jnp.float32)
    for q in range(patches):
        piece = slice(q * GRAIN, (q + 1) * GRAIN)
        mix[piece, :] = jnp.where(same, wide[piece], 0.0).astype(jnp.bfloat16)

    def sums(i):
        load(i).wait()
        for b in range(rows // GRAIN):
            piece = pl.ds(pl.multiple_of(others[steps[i]] * rows + b * GRAIN, GRAIN), GRAIN)
            got = jnp.dot(mix[...], tbuf[:, piece, :].reshape(count * GRAIN, side), preferred_element_type=jnp.float32)
            got = got.reshape(2, chips, GRAIN, side)
            give[:, piece, :] = got[0].astype(jnp.bfloat16)
            keep[:, piece, :] = got[1]

    def whole(i, j):
        total = keep[j, span(i), :] + half[j, span(i), :].astype(jnp.float32)
        return total + near_in[j].astype(jnp.float32) if i == own else total

    def send_near():
        core_copy(first).wait_recv()

        def one(j):
            near[j] = whole(first, j).astype(jnp.bfloat16)

        loop(0, chips, one)
        near_copy().start()

    def send_chips(i):
        core_copy(i).wait_recv()
        if i == own:
            near_copy().wait_recv()

        def one(o):
            chip_sum[o - 1, span(i), :] = whole(i, chip_at(o)).astype(jnp.bfloat16)
            chip_copy(o, i).start()

        loop(1, chips, one)

    def gather(i):
        piece = span(i)
        mine[...] = whole(i, k)

        def one(o):
            chip_copy(o, i).wait_recv()
            mine[...] += inbox[o - 1, piece, :].astype(jnp.float32)

        loop(1, chips, one)

    sums(0)
    pl.semaphore_wait(barrier, 1 + chips - 1 + visits - 1)
    core_copy(0).start()
    named = jnp.where(routes[...] == lax.broadcasted_iota(jnp.int32, (patches, count), 0), scales, 0.0)
    tot[...] = jnp.dot(named.astype(jnp.bfloat16), jnp.ones((count, 128), jnp.bfloat16), preferred_element_type=jnp.float32)
    tot_core_copy().start()
    def total_of_plane():
        tot_core[...] = tot_chip[...]

        def add_plane(o):
            tot_plane_copy(o).wait_recv()
            tot_core[...] += tot_plane[o - 1]

        loop(1, chips, add_plane)
        loop(1, visits, lambda o: tot_lane_copy(o).start())

    def total_of_lane():
        tot[...] = tot_core[...]

        def add_lane(o):
            tot_lane_copy(o).wait_recv()
            tot[...] += tot_lane[o - 1]

        loop(1, visits, add_lane)

    for i in range(1, visits):
        sums(i)
        core_copy(i).start()
        if i == 1:
            tot_core_copy().wait()
            tot_chip[...] = tot[...] + tot_core[...]
            loop(1, chips, lambda o: tot_plane_copy(o).start())
        if i - 1 == first:
            send_near()
        else:
            send_chips(i - 1)

    total_of_plane()
    for n in farther:
        if n == farther[-1]:
            send_chips(own)
        gather(n)
        lane_sum[steps[n] - 2] = mine[...].astype(jnp.bfloat16)
        lane_copy(steps[n]).start()
    gather(own)
    total_of_lane()
    for o in range(visits - 1, 1, -1):
        lane_copy(o).wait_recv()
        mine[...] += lane_in[o - 2].astype(jnp.float32)
    out[k, c, span(own), :] = (mine[...] / tot[pl.ds(p, 1), :][0:1, 0:1]).astype(jnp.bfloat16)

    def fan_out(n):
        loop(1, chips, lambda o: fan_copy(o, n, k).start())

    def forward(n):
        loop(1, chips, lambda o: fan_copy(o, n, chip_at(o)).wait_recv())
        pair_copy(n, c).start()

    back = [steps.index(o) for o in range(1, visits)]
    for o in range(1, visits):
        back_copy(o, own).start()
    fan_out(own)
    for n in units:
        core_copy(n).wait_send()
        if n != first:
            loop(1, chips, lambda o: chip_copy(o, n).wait_send())
    near_copy().wait_send()
    for o in range(2, visits):
        lane_copy(o).wait_send()
    loop(1, visits, lambda o: tot_lane_copy(o).wait_send())
    loop(1, chips, lambda o: tot_plane_copy(o).wait_send())
    for o in range(1, visits):
        if o == visits - 1:
            forward(own)
        back_copy(o, back[o - 1]).wait_recv()
        fan_out(back[o - 1])
    for n in back:
        forward(n)
    for o in range(1, visits):
        back_copy(o, own).wait_send()
    for n in units:
        loop(1, chips, lambda o: fan_copy(o, n, k).wait_send())
    for n in units:
        pair_copy(n, c).wait_send()
    for n in units:
        pair_copy(n, 1 - c).wait_recv()


def coadds(tiles, weights, routes, patches, visits):
    count, side, _ = tiles.shape
    chips = patches // 2
    rows = side // visits
    dma = pltpu.SemaphoreType.DMA
    block = pl.BlockSpec(memory_space=pltpu.VMEM)
    far = pl.BlockSpec(memory_space=pltpu.HBM)
    lane = max(visits - 2, 1)
    peer = max(chips - 1, 1)
    bf16, f32 = jnp.bfloat16, jnp.float32
    return pl.pallas_call(
        functools.partial(coadd_kernel, chips, visits),
        in_specs=[far, far, far],
        out_specs=block,
        out_shape=jax.ShapeDtypeStruct((chips, 2, side, side), bf16),
        scratch_shapes=[
            pltpu.VMEM(routes.shape, routes.dtype),
            pltpu.VMEM(weights.shape, weights.dtype),
            pltpu.VMEM((count, side, side), bf16),
            pltpu.VMEM((patches * GRAIN, count * GRAIN), bf16),
            pltpu.VMEM((chips, side, side), bf16),
            pltpu.VMEM((chips, side, side), f32),
            pltpu.VMEM((chips, side, side), bf16),
            pltpu.VMEM((peer, side, side), bf16),
            pltpu.VMEM((peer, side, side), bf16),
            pltpu.VMEM((rows, side), f32),
            pltpu.VMEM((chips, rows, side), bf16),
            pltpu.VMEM((chips, rows, side), bf16),
            pltpu.VMEM((lane, rows, side), bf16),
            pltpu.VMEM((lane, rows, side), bf16),
            pltpu.VMEM((patches, 128), f32),
            pltpu.VMEM((patches, 128), f32),
            pltpu.VMEM((patches, 128), f32),
            pltpu.VMEM((peer, patches, 128), f32),
            pltpu.VMEM((visits - 1, patches, 128), f32),
            dma((2,)), dma((visits,)), dma((visits,)), dma((visits,)), dma((peer, visits)), dma((peer, visits)), dma, dma,
            dma((lane,)), dma((lane,)), dma((visits - 1,)), dma((visits - 1,)), dma((peer, visits)), dma((peer, visits)),
            dma((visits,)), dma((visits,)), dma, dma, dma((peer,)), dma((peer,)), dma((visits - 1,)), dma((visits - 1,)),
        ],
        compiler_params=pltpu.CompilerParams(collective_id=0, has_side_effects=True, vmem_limit_bytes=40 << 20),
        name="coadds",
    )(*(pltpu.with_memory_space_constraint(x, pltpu.HBM) for x in (routes, weights, tiles)))


def band(row):
    half = 128
    ring = pltpu.roll(jnp.broadcast_to(row, (half, half)), 0, 1, stride=1, stride_axis=0)
    gap = lax.broadcasted_iota(jnp.int32, (half, half), 1) - lax.broadcasted_iota(jnp.int32, (half, half), 0)
    zero = jnp.zeros_like(ring)
    near = jnp.where((gap < 64) & (gap > -64), ring, zero).astype(jnp.bfloat16)
    upper = jnp.where(gap <= -64, ring, zero).astype(jnp.bfloat16)
    lower = jnp.where(gap >= 64, ring, zero).astype(jnp.bfloat16)
    return jnp.concatenate(
        [jnp.concatenate([near, upper], axis=1), jnp.concatenate([lower, near], axis=1)], axis=0
    )


def match_kernel(kernel, group, routes, taps, tiles, coadd, out, own, rings, ready, sent, own_sent):
    count, side, _ = tiles.shape
    tap = lax.broadcasted_iota(jnp.int32, (kernel, 128), 0)
    lane = lax.broadcasted_iota(jnp.int32, (kernel, 128), 1)
    reach = kernel // 2
    gap = jnp.where(lane >= 64, lane - 128, lane)
    mine = pltpu.make_async_copy(coadd.at[lax.axis_index("patch")], own.at[0], own_sent)
    mine.start()
    for side_, hot in enumerate((tap == reach + gap, tap == reach - gap)):
        rings[side_] = lax.dot_general(
            taps[:, side_, :], hot.astype(jnp.float32).astype(jnp.bfloat16), (((0,), (0,)), ((), ())),
            preferred_element_type=jnp.float32)

    def send(g):
        piece = pl.ds(g * group, group)
        return pltpu.make_async_copy(ready.at[piece], out.at[piece], sent.at[g])

    def rows(g):
        return [
            jnp.dot(band(rings[0, place : place + 1, :]), coadd[routes[place]],
                    preferred_element_type=jnp.float32).astype(jnp.bfloat16)
            for place in range(g * group, (g + 1) * group)]

    passes = rows(0)
    for g in range(count // group):
        later = rows(g + 1) if False and g + 1 < count // group else None
        for i in range(group):
            place = g * group + i
            template = jnp.dot(passes[i], band(rings[1, place : place + 1, :]),
                               preferred_element_type=jnp.float32).astype(jnp.bfloat16)
            ready[place] = tiles[place] - template
        send(g).start()
        if g + 1 < count // group:
            passes = later if False else rows(g + 1)
    for g in range(count // group):
        send(g).wait()
    mine.wait()


def subtract(tiles, taps, routes, coadd, group):
    count, side, _ = tiles.shape
    kernel = taps.shape[2]
    block = pl.BlockSpec(memory_space=pltpu.VMEM)
    return pl.pallas_call(
        functools.partial(match_kernel, kernel, group),
        in_specs=[pl.BlockSpec(memory_space=pltpu.SMEM), block, block, block],
        out_specs=[pl.BlockSpec(memory_space=pltpu.HBM)] * 2,
        out_shape=[
            pltpu.HBM(tiles.shape, jnp.bfloat16),
            pltpu.HBM((1, side, side), jnp.bfloat16),
        ],
        scratch_shapes=[
            pltpu.VMEM((2, count, 128), jnp.float32),
            pltpu.VMEM(tiles.shape, jnp.bfloat16),
            pltpu.SemaphoreType.DMA((count // group,)),
            pltpu.SemaphoreType.DMA,
        ],
        compiler_params=pltpu.CompilerParams(vmem_limit_bytes=24 << 20),
        name="subtract",
    )(routes, taps.transpose(2, 1, 0), tiles, coadd)


def local(warped_tiles, tile_weights, kernel_taps, patch_routes):
    patches = lax.axis_size("patch")
    side = warped_tiles.shape[1]
    coadd = coadds(warped_tiles, tile_weights[None, :], patch_routes.T, patches, lax.axis_size("visit"))
    return tuple(subtract(warped_tiles, kernel_taps, patch_routes[:, 0], coadd.reshape(patches, side, side), 4))


def solution(mesh):
    in_specs = (
        P(("visit", "patch"), None, None),
        P(("visit", "patch")),
        P(("visit", "patch"), None, None),
        P(("visit", "patch"), None),
    )
    out_specs = (P(("visit", "patch"), None, None), P("patch", None, None))
    return jax.shard_map(local, mesh=mesh, in_specs=in_specs, out_specs=out_specs, check_vma=False)
```

```python
import functools
import jax
import jax.numpy as jnp
from jax import lax
from jax.experimental import pallas as pl
from jax.experimental.pallas import tpu as pltpu
from jax.sharding import PartitionSpec as P

GRAIN = 16


def flip(number, other, size):
    result, bit = 0, 1
    while bit < size:
        mine, its = lax.rem(lax.div(number, bit), 2), other // bit % 2 if isinstance(other, int) else lax.rem(lax.div(other, bit), 2)
        result = result + bit * (mine + its - 2 * mine * its)
        bit *= 2
    return result


def loop(low, high, body):
    if high - low <= 4:
        for i in range(low, high):
            body(i)
    else:
        lax.fori_loop(low, high, lambda i, _: (body(i), 0)[1], 0)


def coadd_kernel(chips, visits, routes_far, weights_far, tiles, out, routes, weights, tbuf, mix, give, keep, half, chip_sum, inbox, mine, near, near_in,
                 lane_sum, lane_in, tot, tot_core, tot_chip, tot_plane, tot_lane,
                 small_s, load_s, core_s, core_r, chip_s, chip_r, near_s, near_r, lane_s, lane_r, back_s, back_r, fan_s, fan_r,
                 pair_s, pair_r, totc_s, totc_r, totp_s, totp_r, totz_s, totz_r):
    v = lax.axis_index("visit")
    p = lax.axis_index("patch")
    k, c = lax.div(p, 2), lax.rem(p, 2)
    patches = 2 * chips
    count, side, _ = tiles.shape
    rows = side // visits
    steps = [visits - 1, 1] + list(range(visits - 2, 1, -1)) + [0]
    first = steps.index(1)
    farther = [n for n in range(visits) if steps[n] > 1]
    others = [flip(v, o, visits) for o in range(visits)]
    units = range(visits)
    own = visits - 1
    sibling = (v, 2 * k + 1 - c)

    def span(n):
        return pl.ds(pl.multiple_of(others[steps[n]] * rows, rows), rows)

    known = {}

    def chip_at(o):
        if not isinstance(o, int):
            return flip(k, o, chips)
        if o not in known:
            known[o] = flip(k, o, chips)
        return known[o]

    def plane_at(o):
        return (v, 2 * chip_at(o) + c)

    def visit_at(o):
        return others[o] if isinstance(o, int) else flip(v, o, visits)

    def remote(src, dst, send, recv, device):
        return pltpu.make_async_remote_copy(
            src_ref=src, dst_ref=dst, send_sem=send, recv_sem=recv,
            device_id=device, device_id_type=pl.DeviceIdType.MESH)

    def load(i):
        piece = span(i)
        return pltpu.make_async_copy(tiles.at[:, piece], tbuf.at[:, piece], load_s.at[i])

    def core_copy(i):
        piece = span(i)
        return remote(give.at[:, piece], half.at[:, piece], core_s.at[i], core_r.at[i], sibling)

    def chip_copy(o, i):
        piece = span(i)
        return remote(chip_sum.at[o - 1, piece], inbox.at[o - 1, piece], chip_s.at[o - 1, i], chip_r.at[o - 1, i], plane_at(o))

    def near_copy(part):
        piece = pl.ds(0, 1) if part else pl.ds(1, chips - 1)
        return remote(near.at[piece], near_in.at[piece], near_s.at[part], near_r.at[part], (others[1], p))

    def lane_copy(o):
        return remote(lane_sum.at[o - 2], lane_in.at[o - 2], lane_s.at[o - 2], lane_r.at[o - 2], (others[o], p))

    def back_copy(o, n):
        piece = out.at[k, c, span(n)]
        return remote(piece, piece, back_s.at[o - 1], back_r.at[o - 1], (others[o], p))

    def fan_copy(o, i, chip):
        piece = out.at[chip, c, span(i)]
        return remote(piece, piece, fan_s.at[o - 1, i], fan_r.at[o - 1, i], plane_at(o))

    def pair_copy(i, core):
        piece = out.at[:, core, span(i)]
        return remote(piece, piece, pair_s.at[i], pair_r.at[i], sibling)

    def tot_core_copy():
        return remote(tot, tot_core, totc_s, totc_r, sibling)

    def tot_plane_copy(o):
        return remote(tot_chip, tot_plane.at[o - 1], totp_s.at[o - 1], totp_r.at[o - 1], plane_at(o))

    def tot_lane_copy(o):
        return remote(tot_core, tot_lane.at[o - 1], totz_s.at[o - 1], totz_r.at[o - 1], (visit_at(o), p))

    barrier = pltpu.get_barrier_semaphore()

    def greet(device):
        pl.semaphore_signal(barrier, inc=1, device_id=device, device_id_type=pl.DeviceIdType.MESH)

    small = [pltpu.make_async_copy(routes_far, routes, small_s.at[0]),
             pltpu.make_async_copy(weights_far, weights, small_s.at[1])]
    for copy in small:
        copy.start()
    for o in range(chips if chips <= 4 else 1):
        chip_at(o)
    for i in units:
        load(i).start()
    greet(sibling)
    loop(1, chips, lambda o: greet(plane_at(o)))
    loop(1, visits, lambda o: greet((visit_at(o), p)))

    slot = lax.shift_right_logical(lax.broadcasted_iota(jnp.int32, (patches * GRAIN, count), 0), 4)
    patch = jnp.where(slot < chips, 2 * slot + 1 - c, 2 * (slot - chips) + c)
    grain = (count, count * GRAIN)
    widen = (lax.shift_right_logical(lax.broadcasted_iota(jnp.int32, grain, 1), 4)
             == lax.broadcasted_iota(jnp.int32, grain, 0)).astype(jnp.float32).astype(jnp.bfloat16)
    grain = (GRAIN, count * GRAIN)
    same = lax.broadcasted_iota(jnp.int32, grain, 0) == (lax.broadcasted_iota(jnp.int32, grain, 1) & (GRAIN - 1))
    for copy in small:
        copy.wait()
    scales = weights[...].astype(jnp.float32)
    routed = jnp.where(routes[...] == patch, scales, 0.0).astype(jnp.bfloat16)
    wide = jnp.dot(routed, widen, preferred_element_type=jnp.float32)
    for q in range(patches):
        piece = slice(q * GRAIN, (q + 1) * GRAIN)
        mix[piece, :] = jnp.where(same, wide[piece], 0.0).astype(jnp.bfloat16)

    def sums(i):
        load(i).wait()
        for b in range(rows // GRAIN):
            piece = pl.ds(pl.multiple_of(others[steps[i]] * rows + b * GRAIN, GRAIN), GRAIN)
            got = jnp.dot(mix[...], tbuf[:, piece, :].reshape(count * GRAIN, side), preferred_element_type=jnp.float32)
            got = got.reshape(2, chips, GRAIN, side)
            give[:, piece, :] = got[0].astype(jnp.bfloat16)
            keep[:, piece, :] = got[1]

    def whole(i, o):
        j = chip_at(o)
        total = keep[j, span(i), :] + half[j, span(i), :].astype(jnp.float32)
        return total + near_in[o].astype(jnp.float32) if i == own else total

    def send_near():
        core_copy(first).wait_recv()

        def one(o):
            near[o] = whole(first, o).astype(jnp.bfloat16)

        loop(1, chips, one)
        near_copy(0).start()
        one(0)
        near_copy(1).start()

    def send_chips(i):
        core_copy(i).wait_recv()
        if i == own:
            near_copy(0).wait_recv()

        def one(o):
            chip_sum[o - 1, span(i), :] = whole(i, o).astype(jnp.bfloat16)
            chip_copy(o, i).start()

        loop(1, chips, one)

    def gather(i):
        piece = span(i)
        if i == own:
            near_copy(1).wait_recv()
        mine[...] = whole(i, 0)

        def one(o):
            chip_copy(o, i).wait_recv()
            mine[...] += inbox[o - 1, piece, :].astype(jnp.float32)

        loop(1, chips, one)

    sums(0)
    pl.semaphore_wait(barrier, 1 + chips - 1 + visits - 1)
    core_copy(0).start()
    named = jnp.where(routes[...] == lax.broadcasted_iota(jnp.int32, (patches, count), 0), scales, 0.0)
    tot[...] = jnp.dot(named.astype(jnp.bfloat16), jnp.ones((count, 128), jnp.bfloat16), preferred_element_type=jnp.float32)
    tot_core_copy().start()
    def total_of_plane():
        tot_core[...] = tot_chip[...]

        def add_plane(o):
            tot_plane_copy(o).wait_recv()
            tot_core[...] += tot_plane[o - 1]

        loop(1, chips, add_plane)
        loop(1, visits, lambda o: tot_lane_copy(o).start())

    def total_of_lane():
        tot[...] = tot_core[...]

        def add_lane(o):
            tot_lane_copy(o).wait_recv()
            tot[...] += tot_lane[o - 1]

        loop(1, visits, add_lane)

    for i in range(1, visits):
        sums(i)
        core_copy(i).start()
        if i == 1:
            tot_core_copy().wait()
            tot_chip[...] = tot[...] + tot_core[...]
            loop(1, chips, lambda o: tot_plane_copy(o).start())
        if i - 1 == first:
            send_near()
        else:
            send_chips(i - 1)

    total_of_plane()
    for n in farther:
        if n == farther[-1]:
            send_chips(own)
        gather(n)
        lane_sum[steps[n] - 2] = mine[...].astype(jnp.bfloat16)
        lane_copy(steps[n]).start()
    gather(own)
    total_of_lane()
    for o in range(visits - 1, 1, -1):
        lane_copy(o).wait_recv()
        mine[...] += lane_in[o - 2].astype(jnp.float32)
    out[k, c, span(own), :] = (mine[...] / tot[pl.ds(p, 1), :][0:1, 0:1]).astype(jnp.bfloat16)

    def fan_out(n):
        loop(1, chips, lambda o: fan_copy(o, n, k).start())

    def forward(n):
        loop(1, chips, lambda o: fan_copy(o, n, chip_at(o)).wait_recv())
        pair_copy(n, c).start()

    back = [steps.index(o) for o in range(1, visits)]
    for o in range(1, visits):
        back_copy(o, own).start()
    fan_out(own)
    for n in units:
        core_copy(n).wait_send()
        if n != first:
            loop(1, chips, lambda o: chip_copy(o, n).wait_send())
    near_copy(0).wait_send()
    near_copy(1).wait_send()
    for o in range(2, visits):
        lane_copy(o).wait_send()
    loop(1, visits, lambda o: tot_lane_copy(o).wait_send())
    loop(1, chips, lambda o: tot_plane_copy(o).wait_send())
    for o in range(1, visits):
        if o == visits - 1:
            forward(own)
        back_copy(o, back[o - 1]).wait_recv()
        fan_out(back[o - 1])
    for n in back:
        forward(n)
    for o in range(1, visits):
        back_copy(o, own).wait_send()
    for n in units:
        loop(1, chips, lambda o: fan_copy(o, n, k).wait_send())
    for n in units:
        pair_copy(n, c).wait_send()
    for n in units:
        pair_copy(n, 1 - c).wait_recv()


def coadds(tiles, weights, routes, patches, visits):
    count, side, _ = tiles.shape
    chips = patches // 2
    rows = side // visits
    dma = pltpu.SemaphoreType.DMA
    block = pl.BlockSpec(memory_space=pltpu.VMEM)
    far = pl.BlockSpec(memory_space=pltpu.HBM)
    lane = max(visits - 2, 1)
    peer = max(chips - 1, 1)
    bf16, f32 = jnp.bfloat16, jnp.float32
    return pl.pallas_call(
        functools.partial(coadd_kernel, chips, visits),
        in_specs=[far, far, far],
        out_specs=block,
        out_shape=jax.ShapeDtypeStruct((chips, 2, side, side), bf16),
        scratch_shapes=[
            pltpu.VMEM(routes.shape, routes.dtype),
            pltpu.VMEM(weights.shape, weights.dtype),
            pltpu.VMEM((count, side, side), bf16),
            pltpu.VMEM((patches * GRAIN, count * GRAIN), bf16),
            pltpu.VMEM((chips, side, side), bf16),
            pltpu.VMEM((chips, side, side), f32),
            pltpu.VMEM((chips, side, side), bf16),
            pltpu.VMEM((peer, side, side), bf16),
            pltpu.VMEM((peer, side, side), bf16),
            pltpu.VMEM((rows, side), f32),
            pltpu.VMEM((chips, rows, side), bf16),
            pltpu.VMEM((chips, rows, side), bf16),
            pltpu.VMEM((lane, rows, side), bf16),
            pltpu.VMEM((lane, rows, side), bf16),
            pltpu.VMEM((patches, 128), f32),
            pltpu.VMEM((patches, 128), f32),
            pltpu.VMEM((patches, 128), f32),
            pltpu.VMEM((peer, patches, 128), f32),
            pltpu.VMEM((visits - 1, patches, 128), f32),
            dma((2,)), dma((visits,)), dma((visits,)), dma((visits,)), dma((peer, visits)), dma((peer, visits)), dma((2,)), dma((2,)),
            dma((lane,)), dma((lane,)), dma((visits - 1,)), dma((visits - 1,)), dma((peer, visits)), dma((peer, visits)),
            dma((visits,)), dma((visits,)), dma, dma, dma((peer,)), dma((peer,)), dma((visits - 1,)), dma((visits - 1,)),
        ],
        compiler_params=pltpu.CompilerParams(collective_id=0, has_side_effects=True, vmem_limit_bytes=40 << 20),
        name="coadds",
    )(*(pltpu.with_memory_space_constraint(x, pltpu.HBM) for x in (routes, weights, tiles)))


def band(row):
    half = 128
    ring = pltpu.roll(jnp.broadcast_to(row, (half, half)), 0, 1, stride=1, stride_axis=0)
    gap = lax.broadcasted_iota(jnp.int32, (half, half), 1) - lax.broadcasted_iota(jnp.int32, (half, half), 0)
    zero = jnp.zeros_like(ring)
    near = jnp.where((gap < 64) & (gap > -64), ring, zero).astype(jnp.bfloat16)
    upper = jnp.where(gap <= -64, ring, zero).astype(jnp.bfloat16)
    lower = jnp.where(gap >= 64, ring, zero).astype(jnp.bfloat16)
    return jnp.concatenate(
        [jnp.concatenate([near, upper], axis=1), jnp.concatenate([lower, near], axis=1)], axis=0
    )


def match_kernel(kernel, group, routes, taps, tiles, coadd, out, own, rings, ready, sent, own_sent):
    count, side, _ = tiles.shape
    tap = lax.broadcasted_iota(jnp.int32, (kernel, 128), 0)
    lane = lax.broadcasted_iota(jnp.int32, (kernel, 128), 1)
    reach = kernel // 2
    gap = jnp.where(lane >= 64, lane - 128, lane)
    mine = pltpu.make_async_copy(coadd.at[lax.axis_index("patch")], own.at[0], own_sent)
    mine.start()
    for side_, hot in enumerate((tap == reach + gap, tap == reach - gap)):
        rings[side_] = lax.dot_general(
            taps[:, side_, :], hot.astype(jnp.float32).astype(jnp.bfloat16), (((0,), (0,)), ((), ())),
            preferred_element_type=jnp.float32)

    def send(g):
        piece = pl.ds(g * group, group)
        return pltpu.make_async_copy(ready.at[piece], out.at[piece], sent.at[g])

    def rows(g):
        return [
            jnp.dot(band(rings[0, place : place + 1, :]), coadd[routes[place]],
                    preferred_element_type=jnp.float32).astype(jnp.bfloat16)
            for place in range(g * group, (g + 1) * group)]

    passes = rows(0)
    for g in range(count // group):
        later = rows(g + 1) if False and g + 1 < count // group else None
        for i in range(group):
            place = g * group + i
            template = jnp.dot(passes[i], band(rings[1, place : place + 1, :]),
                               preferred_element_type=jnp.float32).astype(jnp.bfloat16)
            ready[place] = tiles[place] - template
        send(g).start()
        if g + 1 < count // group:
            passes = later if False else rows(g + 1)
    for g in range(count // group):
        send(g).wait()
    mine.wait()


def subtract(tiles, taps, routes, coadd, group):
    count, side, _ = tiles.shape
    kernel = taps.shape[2]
    block = pl.BlockSpec(memory_space=pltpu.VMEM)
    return pl.pallas_call(
        functools.partial(match_kernel, kernel, group),
        in_specs=[pl.BlockSpec(memory_space=pltpu.SMEM), block, block, block],
        out_specs=[pl.BlockSpec(memory_space=pltpu.HBM)] * 2,
        out_shape=[
            pltpu.HBM(tiles.shape, jnp.bfloat16),
            pltpu.HBM((1, side, side), jnp.bfloat16),
        ],
        scratch_shapes=[
            pltpu.VMEM((2, count, 128), jnp.float32),
            pltpu.VMEM(tiles.shape, jnp.bfloat16),
            pltpu.SemaphoreType.DMA((count // group,)),
            pltpu.SemaphoreType.DMA,
        ],
        compiler_params=pltpu.CompilerParams(vmem_limit_bytes=24 << 20),
        name="subtract",
    )(routes, taps.transpose(2, 1, 0), tiles, coadd)


def local(warped_tiles, tile_weights, kernel_taps, patch_routes):
    patches = lax.axis_size("patch")
    side = warped_tiles.shape[1]
    coadd = coadds(warped_tiles, tile_weights[None, :], patch_routes.T, patches, lax.axis_size("visit"))
    return tuple(subtract(warped_tiles, kernel_taps, patch_routes[:, 0], coadd.reshape(patches, side, side), 4))


def solution(mesh):
    in_specs = (
        P(("visit", "patch"), None, None),
        P(("visit", "patch")),
        P(("visit", "patch"), None, None),
        P(("visit", "patch"), None),
    )
    out_specs = (P(("visit", "patch"), None, None), P("patch", None, None))
    return jax.shard_map(local, mesh=mesh, in_specs=in_specs, out_specs=out_specs, check_vma=False)
```

```python
import functools
import jax
import jax.numpy as jnp
from jax import lax
from jax.experimental import pallas as pl
from jax.experimental.pallas import tpu as pltpu
from jax.sharding import PartitionSpec as P

GRAIN = 16


def flip(number, other, size):
    result, bit = 0, 1
    while bit < size:
        mine, its = lax.rem(lax.div(number, bit), 2), other // bit % 2 if isinstance(other, int) else lax.rem(lax.div(other, bit), 2)
        result = result + bit * (mine + its - 2 * mine * its)
        bit *= 2
    return result


def loop(low, high, body):
    if high - low <= 4:
        for i in range(low, high):
            body(i)
    else:
        lax.fori_loop(low, high, lambda i, _: (body(i), 0)[1], 0)


def coadd_kernel(chips, visits, routes_far, weights_far, tiles, out, routes, weights, tbuf, mix, give, keep, half, chip_sum, inbox, mine, near, near_in,
                 lane_sum, lane_in, tot, tot_core, tot_chip, tot_plane, tot_lane,
                 small_s, load_s, core_s, core_r, chip_s, chip_r, near_s, near_r, lane_s, lane_r, back_s, back_r, fan_s, fan_r,
                 pair_s, pair_r, totc_s, totc_r, totp_s, totp_r, totz_s, totz_r):
    v = lax.axis_index("visit")
    p = lax.axis_index("patch")
    k, c = lax.div(p, 2), lax.rem(p, 2)
    patches = 2 * chips
    count, side, _ = tiles.shape
    rows = side // visits
    steps = [visits - 1, 1] + list(range(visits - 2, 1, -1)) + [0]
    first = steps.index(1)
    farther = [n for n in range(visits) if steps[n] > 1]
    others = [flip(v, o, visits) for o in range(visits)]
    units = range(visits)
    own = visits - 1
    sibling = (v, 2 * k + 1 - c)

    def span(n):
        return pl.ds(pl.multiple_of(others[steps[n]] * rows, rows), rows)

    known = {}

    def chip_at(o):
        if not isinstance(o, int):
            return flip(k, o, chips)
        if o not in known:
            known[o] = flip(k, o, chips)
        return known[o]

    def plane_at(o):
        return (v, 2 * chip_at(o) + c)

    def visit_at(o):
        return others[o] if isinstance(o, int) else flip(v, o, visits)

    def remote(src, dst, send, recv, device):
        return pltpu.make_async_remote_copy(
            src_ref=src, dst_ref=dst, send_sem=send, recv_sem=recv,
            device_id=device, device_id_type=pl.DeviceIdType.MESH)

    def load(i):
        piece = span(i)
        return pltpu.make_async_copy(tiles.at[:, piece], tbuf.at[:, piece], load_s.at[i])

    def core_copy(i):
        piece = span(i)
        return remote(give.at[:, piece], half.at[:, piece], core_s.at[i], core_r.at[i], sibling)

    def chip_copy(o, i):
        piece = span(i)
        return remote(chip_sum.at[o - 1, piece], inbox.at[o - 1, piece], chip_s.at[o - 1, i], chip_r.at[o - 1, i], plane_at(o))

    def near_copy(part):
        piece = pl.ds(0, 1) if part else pl.ds(1, chips - 1)
        return remote(near.at[piece], near_in.at[piece], near_s.at[part], near_r.at[part], (others[1], p))

    def lane_copy(o):
        return remote(lane_sum.at[o - 2], lane_in.at[o - 2], lane_s.at[o - 2], lane_r.at[o - 2], (others[o], p))

    def back_copy(o, n):
        piece = out.at[k, c, span(n)]
        return remote(piece, piece, back_s.at[o - 1], back_r.at[o - 1], (others[o], p))

    def fan_copy(o, i, chip):
        piece = out.at[chip, c, span(i)]
        return remote(piece, piece, fan_s.at[o - 1, i], fan_r.at[o - 1, i], plane_at(o))

    def pair_copy(i, core):
        piece = out.at[:, core, span(i)]
        return remote(piece, piece, pair_s.at[i], pair_r.at[i], sibling)

    def tot_core_copy():
        return remote(tot, tot_core, totc_s, totc_r, sibling)

    def tot_plane_copy(o):
        return remote(tot_chip, tot_plane.at[o - 1], totp_s.at[o - 1], totp_r.at[o - 1], plane_at(o))

    def tot_lane_copy(o):
        return remote(tot_core, tot_lane.at[o - 1], totz_s.at[o - 1], totz_r.at[o - 1], (visit_at(o), p))

    barrier = pltpu.get_barrier_semaphore()

    def greet(device):
        pl.semaphore_signal(barrier, inc=1, device_id=device, device_id_type=pl.DeviceIdType.MESH)

    small = [pltpu.make_async_copy(routes_far, routes, small_s.at[0]),
             pltpu.make_async_copy(weights_far, weights, small_s.at[1])]
    for copy in small:
        copy.start()
    for o in range(chips if chips <= 4 else 1):
        chip_at(o)
    for i in units:
        load(i).start()
    greet(sibling)
    loop(1, chips, lambda o: greet(plane_at(o)))
    loop(1, visits, lambda o: greet((visit_at(o), p)))

    slot = lax.shift_right_logical(lax.broadcasted_iota(jnp.int32, (patches * GRAIN, count), 0), 4)
    patch = jnp.where(slot < chips, 2 * slot + 1 - c, 2 * (slot - chips) + c)
    grain = (count, count * GRAIN)
    widen = (lax.shift_right_logical(lax.broadcasted_iota(jnp.int32, grain, 1), 4)
             == lax.broadcasted_iota(jnp.int32, grain, 0)).astype(jnp.float32).astype(jnp.bfloat16)
    grain = (GRAIN, count * GRAIN)
    same = lax.broadcasted_iota(jnp.int32, grain, 0) == (lax.broadcasted_iota(jnp.int32, grain, 1) & (GRAIN - 1))
    for copy in small:
        copy.wait()
    scales = weights[...].astype(jnp.float32)
    routed = jnp.where(routes[...] == patch, scales, 0.0).astype(jnp.bfloat16)
    wide = jnp.dot(routed, widen, preferred_element_type=jnp.float32)
    for q in range(patches):
        piece = slice(q * GRAIN, (q + 1) * GRAIN)
        mix[piece, :] = jnp.where(same, wide[piece], 0.0).astype(jnp.bfloat16)

    def sums(i):
        load(i).wait()
        for b in range(rows // GRAIN):
            piece = pl.ds(pl.multiple_of(others[steps[i]] * rows + b * GRAIN, GRAIN), GRAIN)
            got = jnp.dot(mix[...], tbuf[:, piece, :].reshape(count * GRAIN, side), preferred_element_type=jnp.float32)
            got = got.reshape(2, chips, GRAIN, side)
            give[:, piece, :] = got[0].astype(jnp.bfloat16)
            keep[:, piece, :] = got[1]

    def whole(i, o):
        j = chip_at(o)
        total = keep[j, span(i), :] + half[j, span(i), :].astype(jnp.float32)
        return total + near_in[o].astype(jnp.float32) if i == own else total

    def send_near():
        core_copy(first).wait_recv()

        def one(o):
            near[o] = whole(first, o).astype(jnp.bfloat16)

        loop(1, chips, one)
        near_copy(0).start()
        one(0)
        near_copy(1).start()

    def send_chips(i):
        core_copy(i).wait_recv()
        if i == own:
            near_copy(0).wait_recv()

        def one(o):
            chip_sum[o - 1, span(i), :] = whole(i, o).astype(jnp.bfloat16)
            chip_copy(o, i).start()

        loop(1, chips, one)

    def gather(i):
        piece = span(i)
        if i == own:
            near_copy(1).wait_recv()
        mine[...] = whole(i, 0)

        def one(o):
            chip_copy(o, i).wait_recv()
            mine[...] += inbox[o - 1, piece, :].astype(jnp.float32)

        loop(1, chips, one)

    sums(0)
    pl.semaphore_wait(barrier, 1 + chips - 1 + visits - 1)
    core_copy(0).start()
    named = jnp.where(routes[...] == lax.broadcasted_iota(jnp.int32, (patches, count), 0), scales, 0.0)
    tot[...] = jnp.dot(named.astype(jnp.bfloat16), jnp.ones((count, 128), jnp.bfloat16), preferred_element_type=jnp.float32)
    tot_core_copy().start()
    def total_of_plane():
        tot_core[...] = tot_chip[...]

        def add_plane(o):
            tot_plane_copy(o).wait_recv()
            tot_core[...] += tot_plane[o - 1]

        loop(1, chips, add_plane)
        loop(1, visits, lambda o: tot_lane_copy(o).start())

    def total_of_lane():
        tot[...] = tot_core[...]

        def add_lane(o):
            tot_lane_copy(o).wait_recv()
            tot[...] += tot_lane[o - 1]

        loop(1, visits, add_lane)

    for i in range(1, visits):
        sums(i)
        core_copy(i).start()
        if i == 1:
            tot_core_copy().wait()
            tot_chip[...] = tot[...] + tot_core[...]
            loop(1, chips, lambda o: tot_plane_copy(o).start())
        if i - 1 == first:
            send_near()
        else:
            send_chips(i - 1)

    total_of_plane()
    for n in farther:
        if n == farther[-1]:
            send_chips(own)
        gather(n)
        lane_sum[steps[n] - 2] = mine[...].astype(jnp.bfloat16)
        lane_copy(steps[n]).start()
    gather(own)
    total_of_lane()
    for o in range(visits - 1, 1, -1):
        lane_copy(o).wait_recv()
        mine[...] += lane_in[o - 2].astype(jnp.float32)
    out[k, c, span(own), :] = (mine[...] / tot[pl.ds(p, 1), :][0:1, 0:1]).astype(jnp.bfloat16)

    def fan_out(n):
        loop(1, chips, lambda o: fan_copy(o, n, k).start())

    def forward(n):
        loop(1, chips, lambda o: fan_copy(o, n, chip_at(o)).wait_recv())
        pair_copy(n, c).start()

    back = [steps.index(o) for o in range(1, visits)]
    for o in range(visits - 1, 0, -1):
        back_copy(o, own).start()
    fan_out(own)
    for n in units:
        core_copy(n).wait_send()
        if n != first:
            loop(1, chips, lambda o: chip_copy(o, n).wait_send())
    near_copy(0).wait_send()
    near_copy(1).wait_send()
    for o in range(2, visits):
        lane_copy(o).wait_send()
    loop(1, visits, lambda o: tot_lane_copy(o).wait_send())
    loop(1, chips, lambda o: tot_plane_copy(o).wait_send())
    for o in range(1, visits):
        if o == visits - 1:
            forward(own)
        back_copy(o, back[o - 1]).wait_recv()
        fan_out(back[o - 1])
    for n in back:
        forward(n)
    for o in range(1, visits):
        back_copy(o, own).wait_send()
    for n in units:
        loop(1, chips, lambda o: fan_copy(o, n, k).wait_send())
    for n in units:
        pair_copy(n, c).wait_send()
    for n in units:
        pair_copy(n, 1 - c).wait_recv()


def coadds(tiles, weights, routes, patches, visits):
    count, side, _ = tiles.shape
    chips = patches // 2
    rows = side // visits
    dma = pltpu.SemaphoreType.DMA
    block = pl.BlockSpec(memory_space=pltpu.VMEM)
    far = pl.BlockSpec(memory_space=pltpu.HBM)
    lane = max(visits - 2, 1)
    peer = max(chips - 1, 1)
    bf16, f32 = jnp.bfloat16, jnp.float32
    return pl.pallas_call(
        functools.partial(coadd_kernel, chips, visits),
        in_specs=[far, far, far],
        out_specs=block,
        out_shape=jax.ShapeDtypeStruct((chips, 2, side, side), bf16),
        scratch_shapes=[
            pltpu.VMEM(routes.shape, routes.dtype),
            pltpu.VMEM(weights.shape, weights.dtype),
            pltpu.VMEM((count, side, side), bf16),
            pltpu.VMEM((patches * GRAIN, count * GRAIN), bf16),
            pltpu.VMEM((chips, side, side), bf16),
            pltpu.VMEM((chips, side, side), f32),
            pltpu.VMEM((chips, side, side), bf16),
            pltpu.VMEM((peer, side, side), bf16),
            pltpu.VMEM((peer, side, side), bf16),
            pltpu.VMEM((rows, side), f32),
            pltpu.VMEM((chips, rows, side), bf16),
            pltpu.VMEM((chips, rows, side), bf16),
            pltpu.VMEM((lane, rows, side), bf16),
            pltpu.VMEM((lane, rows, side), bf16),
            pltpu.VMEM((patches, 128), f32),
            pltpu.VMEM((patches, 128), f32),
            pltpu.VMEM((patches, 128), f32),
            pltpu.VMEM((peer, patches, 128), f32),
            pltpu.VMEM((visits - 1, patches, 128), f32),
            dma((2,)), dma((visits,)), dma((visits,)), dma((visits,)), dma((peer, visits)), dma((peer, visits)), dma((2,)), dma((2,)),
            dma((lane,)), dma((lane,)), dma((visits - 1,)), dma((visits - 1,)), dma((peer, visits)), dma((peer, visits)),
            dma((visits,)), dma((visits,)), dma, dma, dma((peer,)), dma((peer,)), dma((visits - 1,)), dma((visits - 1,)),
        ],
        compiler_params=pltpu.CompilerParams(collective_id=0, has_side_effects=True, vmem_limit_bytes=40 << 20),
        name="coadds",
    )(*(pltpu.with_memory_space_constraint(x, pltpu.HBM) for x in (routes, weights, tiles)))


def band(row):
    half = 128
    ring = pltpu.roll(jnp.broadcast_to(row, (half, half)), 0, 1, stride=1, stride_axis=0)
    gap = lax.broadcasted_iota(jnp.int32, (half, half), 1) - lax.broadcasted_iota(jnp.int32, (half, half), 0)
    zero = jnp.zeros_like(ring)
    near = jnp.where((gap < 64) & (gap > -64), ring, zero).astype(jnp.bfloat16)
    upper = jnp.where(gap <= -64, ring, zero).astype(jnp.bfloat16)
    lower = jnp.where(gap >= 64, ring, zero).astype(jnp.bfloat16)
    return jnp.concatenate(
        [jnp.concatenate([near, upper], axis=1), jnp.concatenate([lower, near], axis=1)], axis=0
    )


def match_kernel(kernel, group, routes, taps, tiles, coadd, out, own, rings, ready, sent, own_sent):
    count, side, _ = tiles.shape
    tap = lax.broadcasted_iota(jnp.int32, (kernel, 128), 0)
    lane = lax.broadcasted_iota(jnp.int32, (kernel, 128), 1)
    reach = kernel // 2
    gap = jnp.where(lane >= 64, lane - 128, lane)
    mine = pltpu.make_async_copy(coadd.at[lax.axis_index("patch")], own.at[0], own_sent)
    mine.start()
    for side_, hot in enumerate((tap == reach + gap, tap == reach - gap)):
        rings[side_] = lax.dot_general(
            taps[:, side_, :], hot.astype(jnp.float32).astype(jnp.bfloat16), (((0,), (0,)), ((), ())),
            preferred_element_type=jnp.float32)

    def send(g):
        piece = pl.ds(g * group, group)
        return pltpu.make_async_copy(ready.at[piece], out.at[piece], sent.at[g])

    def rows(g):
        return [
            jnp.dot(band(rings[0, place : place + 1, :]), coadd[routes[place]],
                    preferred_element_type=jnp.float32).astype(jnp.bfloat16)
            for place in range(g * group, (g + 1) * group)]

    passes = rows(0)
    for g in range(count // group):
        later = rows(g + 1) if False and g + 1 < count // group else None
        for i in range(group):
            place = g * group + i
            template = jnp.dot(passes[i], band(rings[1, place : place + 1, :]),
                               preferred_element_type=jnp.float32).astype(jnp.bfloat16)
            ready[place] = tiles[place] - template
        send(g).start()
        if g + 1 < count // group:
            passes = later if False else rows(g + 1)
    for g in range(count // group):
        send(g).wait()
    mine.wait()


def subtract(tiles, taps, routes, coadd, group):
    count, side, _ = tiles.shape
    kernel = taps.shape[2]
    block = pl.BlockSpec(memory_space=pltpu.VMEM)
    return pl.pallas_call(
        functools.partial(match_kernel, kernel, group),
        in_specs=[pl.BlockSpec(memory_space=pltpu.SMEM), block, block, block],
        out_specs=[pl.BlockSpec(memory_space=pltpu.HBM)] * 2,
        out_shape=[
            pltpu.HBM(tiles.shape, jnp.bfloat16),
            pltpu.HBM((1, side, side), jnp.bfloat16),
        ],
        scratch_shapes=[
            pltpu.VMEM((2, count, 128), jnp.float32),
            pltpu.VMEM(tiles.shape, jnp.bfloat16),
            pltpu.SemaphoreType.DMA((count // group,)),
            pltpu.SemaphoreType.DMA,
        ],
        compiler_params=pltpu.CompilerParams(vmem_limit_bytes=24 << 20),
        name="subtract",
    )(routes, taps.transpose(2, 1, 0), tiles, coadd)


def local(warped_tiles, tile_weights, kernel_taps, patch_routes):
    patches = lax.axis_size("patch")
    side = warped_tiles.shape[1]
    coadd = coadds(warped_tiles, tile_weights[None, :], patch_routes.T, patches, lax.axis_size("visit"))
    return tuple(subtract(warped_tiles, kernel_taps, patch_routes[:, 0], coadd.reshape(patches, side, side), 4))


def solution(mesh):
    in_specs = (
        P(("visit", "patch"), None, None),
        P(("visit", "patch")),
        P(("visit", "patch"), None, None),
        P(("visit", "patch"), None),
    )
    out_specs = (P(("visit", "patch"), None, None), P("patch", None, None))
    return jax.shard_map(local, mesh=mesh, in_specs=in_specs, out_specs=out_specs, check_vma=False)
```
